512 devices in a mesh: ctx: 32 (over z, x_hi), head: 16 (over y, x_lo, core).
Axes of the slice: x: 4 (x_hi: 2, x_lo: 2; x = x_hi * 2 + x_lo), y: 4, z: 16, core: 2. Of those that a mesh axis runs over, the one named last changes fastest.
Arguments:
- query: bfloat16 [65536, 4096], P(('ctx', 'head')), may hold values from -6 to 6
- key: bfloat16 [65536, 2048], P(('ctx', 'head')), may hold values from -6 to 6
- value: bfloat16 [65536, 2048], P(('ctx', 'head')), may hold values from -6 to 6
- out_grad: bfloat16 [65536, 4096], P(('ctx', 'head')), may hold values from -6 to 6
- block_mask: int32 [512, 9], replicated, may hold values from 0 to 1, as said below
Outputs:
- query_grad: bfloat16 [65536, 4096], P(('ctx', 'head'))
- key_grad: bfloat16 [65536, 2048], P(('ctx', 'head'))
- value_grad: bfloat16 [65536, 2048], P(('ctx', 'head'))
The draws below stay inside these ranges and needn't reach their ends.
Inputs may be any that keep to these rules, and one draw needn't show every extreme that they name: block_mask[b, 0] is 1 for every block b; block_mask[b, o] = 1 lets query block b attend key block b - o.
All inputs are finite; a program needn't handle non-finite values.
Results may differ from the reference program's by a relative error of at most 0.0095.
Values may be sent and summed in bfloat16 or wider, within the bound.
A program may use at most 64 MiB of HBM per device.

```python
import jax
import jax.numpy as jnp
from jax import lax

HQ = 32
KEY_VALUE_HEADS = 16
HEAD_WIDTH = 128
WINDOW = 1024
BLOCK = 128
NOFF = 9
SEQUENCE_TOKENS = 65536
NB = 512


def draw_query(key, part):
    final_output = jnp.clip(jax.random.normal(jax.random.fold_in(key, 1), (SEQUENCE_TOKENS, HQ * HEAD_WIDTH), jnp.float32), -6.0, 6.0)
    return final_output.astype(jnp.bfloat16)


def draw_key(key, part):
    final_output = jnp.clip(jax.random.normal(jax.random.fold_in(key, 2), (SEQUENCE_TOKENS, KEY_VALUE_HEADS * HEAD_WIDTH), jnp.float32), -6.0, 6.0)
    return final_output.astype(jnp.bfloat16)


def draw_block_mask(key, part):
    drawn = (jax.random.randint(jax.random.fold_in(key, 4), (NB, NOFF), 0, 4) < 3).astype(jnp.int32)
    column = jax.lax.broadcasted_iota(jnp.int32, (NB, NOFF), 1)
    return jnp.where(column == 0, 1, drawn).astype(jnp.int32)


def block_scale(key, extent, pieces, low, largest):
    def one(dim, blocks):
        steps = jax.random.uniform(jax.random.fold_in(jax.random.fold_in(key, 6), dim), (blocks,), jnp.float32, low / len(pieces), largest / len(pieces))
        return jnp.repeat(jnp.exp(steps), extent[dim] // blocks).reshape((-1,) + (1,) * (len(extent) - dim - 1))

    loudness = one(*pieces[0])
    for cut in pieces[1:]:
        loudness = loudness * one(*cut)
    return loudness


def normal_values(stream_key, shape, deviation, limit, pieces=(), kind=jnp.bfloat16):
    values = deviation * jax.random.normal(stream_key, shape, jnp.float32)
    if pieces:
        values = values * block_scale(stream_key, shape, pieces, -0.22, 0.18)
    return jnp.clip(values, -limit, limit).astype(kind)


def setup_inputs(seed: int = 0) -> dict:
    arg_keys = jax.random.split(jax.random.key(seed), 6)
    return {
        "query": draw_query(jax.random.fold_in(arg_keys[5], 71), 0),
        "key": draw_key(jax.random.fold_in(arg_keys[5], 71), 0),
        "value": normal_values(arg_keys[2], (SEQUENCE_TOKENS, KEY_VALUE_HEADS * HEAD_WIDTH), 1.0, 6.0, ((0, 512),)),
        "out_grad": normal_values(arg_keys[3], (SEQUENCE_TOKENS, HQ * HEAD_WIDTH), 1.0, 6.0, ((0, 512),)),
        "block_mask": draw_block_mask(jax.random.fold_in(arg_keys[5], 71), 0),
    }


PRE_SCALE = 168.0 ** -0.5


def allowed_mask(mask_rows, n_query, n_key, key_lead, key_first):
    q_index = lax.broadcasted_iota(jnp.int32, (n_query, n_key), 0)
    k_index = lax.broadcasted_iota(jnp.int32, (n_query, n_key), 1)
    gap = key_lead + q_index - k_index
    inside = (gap >= 0) & (gap < WINDOW) & (key_first + k_index >= 0)
    q_blocks = n_query // BLOCK
    k_blocks = n_key // BLOCK
    offsets = mask_rows.shape[1]
    a_index = lax.broadcasted_iota(jnp.int32, (q_blocks, k_blocks, offsets), 0)
    b_index = lax.broadcasted_iota(jnp.int32, (q_blocks, k_blocks, offsets), 1)
    o_index = lax.broadcasted_iota(jnp.int32, (q_blocks, k_blocks, offsets), 2)
    picked = jnp.where(o_index == a_index - b_index + key_lead // BLOCK, mask_rows[:, None, :], 0)
    active = jnp.sum(picked, axis=2) > 0
    active = jnp.repeat(jnp.repeat(active, BLOCK, axis=0), BLOCK, axis=1)
    return inside & active


def scores_of(q_part, k_part, allowed):
    n_query = q_part.shape[0]
    n_key = k_part.shape[0]
    kv_groups = k_part.shape[1] // HEAD_WIDTH
    q_heads = q_part.astype(jnp.float32).reshape(n_query, kv_groups, -1, HEAD_WIDTH)
    k_heads = k_part.astype(jnp.float32).reshape(n_key, kv_groups, HEAD_WIDTH)
    raw_scores = jnp.einsum("qgrd,kgd->grqk", q_heads, k_heads) * PRE_SCALE
    return jnp.where(allowed, raw_scores, -jnp.inf)


def tile_pass(q_part, g_part, k_part, v_part, allowed):
    n_query = q_part.shape[0]
    n_key = k_part.shape[0]
    kv_groups = k_part.shape[1] // HEAD_WIDTH
    scores = scores_of(q_part, k_part, allowed)
    row_max = jnp.max(scores, axis=3, keepdims=True)
    row_total = jnp.sum(jnp.exp(scores - row_max), axis=3, keepdims=True)
    log_total = row_max + jnp.log(row_total)
    probs = jnp.exp(scores - log_total)
    probs_low = probs.astype(jnp.bfloat16).astype(jnp.float32)
    q_heads = q_part.astype(jnp.float32).reshape(n_query, kv_groups, -1, HEAD_WIDTH)
    g_heads = g_part.astype(jnp.float32).reshape(n_query, kv_groups, -1, HEAD_WIDTH)
    k_heads = k_part.astype(jnp.float32).reshape(n_key, kv_groups, HEAD_WIDTH)
    v_heads = v_part.astype(jnp.float32).reshape(n_key, kv_groups, HEAD_WIDTH)
    attended = jnp.einsum("grqk,kgd->qgrd", probs_low, v_heads)
    delta = jnp.transpose(jnp.sum(g_heads * attended, axis=3), (1, 2, 0))
    d_value = jnp.einsum("grqk,qgrd->kgd", probs_low, g_heads)
    d_probs = jnp.einsum("qgrd,kgd->grqk", g_heads, v_heads)
    d_scores = (probs * (d_probs - delta[..., None])).astype(jnp.bfloat16).astype(jnp.float32)
    d_query = jnp.einsum("grqk,kgd->qgrd", d_scores, k_heads) * PRE_SCALE
    d_key = jnp.einsum("grqk,qgrd->kgd", d_scores, q_heads) * PRE_SCALE
    return d_query.reshape(n_query, -1), d_key.reshape(n_key, -1), d_value.reshape(n_key, -1)


def reference(query, key, value, out_grad, block_mask):
    seq_len = query.shape[0]
    tile_rows = BLOCK
    n_tiles = seq_len // tile_rows
    zero_rows = jnp.zeros((WINDOW, key.shape[1]), key.dtype)
    k_ext = jnp.concatenate([zero_rows, key], 0)
    v_ext = jnp.concatenate([zero_rows, value], 0)
    span = tile_rows + WINDOW

    def step_fn(state_pair, tile_index):
        d_key_acc, d_value_acc = state_pair
        first_row = (tile_index * tile_rows).astype(jnp.int32)
        q_part = lax.dynamic_slice_in_dim(query, first_row, tile_rows, 0)
        g_part = lax.dynamic_slice_in_dim(out_grad, first_row, tile_rows, 0)
        k_part = lax.dynamic_slice_in_dim(k_ext, first_row, span, 0)
        v_part = lax.dynamic_slice_in_dim(v_ext, first_row, span, 0)
        mask_rows = lax.dynamic_slice_in_dim(block_mask, (first_row // BLOCK).astype(jnp.int32), tile_rows // BLOCK, 0)
        allowed = allowed_mask(mask_rows, tile_rows, span, WINDOW, first_row - WINDOW)
        d_query, d_key, d_value = tile_pass(q_part, g_part, k_part, v_part, allowed)
        d_key_acc = lax.dynamic_update_slice_in_dim(d_key_acc, lax.dynamic_slice_in_dim(d_key_acc, first_row, span, 0) + d_key, first_row, 0)
        d_value_acc = lax.dynamic_update_slice_in_dim(d_value_acc, lax.dynamic_slice_in_dim(d_value_acc, first_row, span, 0) + d_value, first_row, 0)
        return (d_key_acc, d_value_acc), d_query.astype(jnp.bfloat16)

    tile_ids = jnp.arange(n_tiles, dtype=jnp.int32)
    zero_acc = jnp.zeros((seq_len + WINDOW, key.shape[1]), jnp.float32)
    (d_key_ext, d_value_ext), d_query = lax.scan(step_fn, (zero_acc, zero_acc), tile_ids)
    query_grad = d_query.reshape(seq_len, -1)
    key_grad = d_key_ext[WINDOW:].astype(jnp.bfloat16)
    value_grad = d_value_ext[WINDOW:].astype(jnp.bfloat16)
    return (query_grad, key_grad, value_grad)
```

```python
import math

import jax
import jax.numpy as jnp
from jax import lax
from jax.experimental import pallas as pl
from jax.experimental.pallas import tpu as pltpu
from jax.sharding import PartitionSpec as P

HEAD_WIDTH = 128
BLOCK = 128
SPAN_BLOCKS = 9
CHUNK = 3
WINDOW = 1024
PRE_SCALE = 168.0 ** (-0.5)
EXP2_SCALE = PRE_SCALE / math.log(2.0)

F32 = jnp.float32
BF16 = jnp.bfloat16
MESH = pl.DeviceIdType.MESH

NT = (((1,), (1,)), ((), ()))
TN = (((0,), (0,)), ((), ()))
NN = (((1,), (0,)), ((), ()))


def dot(a, b, dims):
    return lax.dot_general(a, b, dims, preferred_element_type=F32)


def fold(x, op):
    return op(x.reshape(BLOCK // 8, 8, x.shape[1]), axis=0)


def bytes_of(ref, sem):
    return pltpu.make_async_copy(ref, ref, sem)


def block_grads(bits, first_row, q2, g2, kv, st, dp, pbs, dss, dk, dv):
    cols = q2.shape[0]
    u_index = lax.broadcasted_iota(jnp.int32, (BLOCK, cols), 0)
    t_index = lax.rem(lax.broadcasted_iota(jnp.int32, (BLOCK, cols), 1), BLOCK)
    causal = u_index <= t_index
    rows = CHUNK * BLOCK

    def span(c):
        return pl.ds(pl.multiple_of(first_row + c * rows, BLOCK), rows)

    m8 = jnp.full((8, cols), -jnp.inf, F32)
    for c in range(SPAN_BLOCKS // CHUNK):
        s = dot(kv[0, span(c), :], q2, NT)
        for i in range(CHUNK):
            o = c * CHUNK + i
            part = s[i * BLOCK : (i + 1) * BLOCK]
            if o == SPAN_BLOCKS - 1:
                part = jnp.where(causal, part, -jnp.inf)
            if o == 0:
                part = jnp.where(causal, -jnp.inf, part)
            st[o] = part
            m8 = jnp.maximum(m8, jnp.where(bits[o], fold(part, jnp.max), -jnp.inf))
    row_max = jnp.max(m8, axis=0, keepdims=True)

    l8 = jnp.zeros((8, cols), F32)
    d8 = jnp.zeros((8, cols), F32)
    for c in range(SPAN_BLOCKS // CHUNK):
        d = dot(kv[1, span(c), :], g2, NT)
        for i in range(CHUNK):
            o = c * CHUNK + i
            part = d[i * BLOCK : (i + 1) * BLOCK]
            shift = jnp.where(bits[o], row_max, jnp.inf)
            e = jnp.exp2((st[o] - shift) * EXP2_SCALE)
            st[o] = e
            dp[o] = part
            l8 += fold(e, jnp.sum)
            d8 += fold(e * part, jnp.sum)
    inverse = 1.0 / jnp.sum(l8, axis=0, keepdims=True)
    delta = jnp.sum(d8, axis=0, keepdims=True) * inverse

    dq = jnp.zeros((cols, HEAD_WIDTH), F32)
    for c in range(SPAN_BLOCKS // CHUNK):
        for i in range(CHUNK):
            o = c * CHUNK + i
            p = st[o] * inverse
            pbs[pl.ds(o * BLOCK, BLOCK), :] = p.astype(BF16)
            dss[pl.ds(o * BLOCK, BLOCK), :] = (p * (dp[o] - delta)).astype(BF16)
        pb = pbs[pl.ds(c * rows, rows), :]
        ds = dss[pl.ds(c * rows, rows), :]
        dv[span(c), :] += dot(pb, g2, NN)
        dk[span(c), :] += dot(ds, q2, NN)
        dq += dot(ds, kv[0, span(c), :], TN)
    return dq * PRE_SCALE


def kernel(
    n_z, q_ref, k_ref, v_ref, g_ref, mask_ref, dq_out, dk_out, dv_out,
    kv, qg, dqs, dkvs, halo_out, halo_in, dk, dv, st, dp, pbs, dss, bits_ref,
    s_q, s_g, s_k, s_v, r_qg, r_kv, s_halo, r_halo, s_back, r_back,
    s_dq, s_dk, s_dv, r_dq, r_dk, r_dv, m_sem,
):
    ctx = lax.axis_index("ctx")
    me_h = lax.axis_index("head")
    z, xh = lax.div(ctx, 2), lax.rem(ctx, 2)
    y, xl, core = lax.div(me_h, 4), lax.rem(lax.div(me_h, 2), 2), lax.rem(me_h, 2)
    x = xh * 2 + xl
    my_head = x * 4 + y
    seg = z * 2 + core
    n_blocks = qg.shape[0]
    half = n_blocks // 2
    other = me_h + 1 - 2 * core
    after = (lax.rem(z + core, n_z) * 2 + xh, other)
    before = (lax.rem(z + n_z - 1 + core, n_z) * 2 + xh, other)

    def target(i):
        pair, second = lax.div(i, 2), lax.rem(i, 2)
        dx, dy = lax.rem(pair, 2) + 2 * second, lax.div(pair, 2)
        tx, ty = lax.rem(x + dx, 4), lax.rem(y + dy, 4)
        return (z * 2 + lax.div(tx, 2), ty * 4 + lax.rem(tx, 2) * 2 + xh), tx * 4 + ty

    def source(i):
        pair, sc = lax.div(i, 2), lax.rem(i, 2)
        dx, dy = lax.rem(pair, 2), lax.div(pair, 2)
        return lax.rem(y + 4 - dy, 4) * 4 + lax.rem(x + dx, 2) * 2 + sc

    rows_mask = pltpu.make_async_copy(
        mask_ref.at[pl.ds(pl.multiple_of(seg * n_blocks, 8), n_blocks), :], bits_ref, m_sem
    )
    rows_mask.start()

    barrier = pltpu.get_barrier_semaphore()

    def greet(i, carry):
        device, _ = target(i)
        pl.semaphore_signal(barrier, inc=1, device_id=device, device_id_type=MESH)
        pl.semaphore_signal(barrier, inc=1, device_id=(seg, i), device_id_type=MESH)
        return carry

    lax.fori_loop(0, n_blocks, greet, 0)
    pl.semaphore_signal(barrier, inc=1, device_id=after, device_id_type=MESH)
    pl.semaphore_signal(barrier, inc=1, device_id=before, device_id_type=MESH)
    pl.semaphore_wait(barrier, 2 * n_blocks + 2)

    mine = xh == core

    def send(is_self, device, src, dst, send_sem, recv_sem):
        @pl.when(is_self)
        def _():
            pltpu.make_async_copy(src, dst, recv_sem).start()

        @pl.when(jnp.logical_not(is_self))
        def _():
            pltpu.make_async_remote_copy(
                src_ref=src, dst_ref=dst, send_sem=send_sem, recv_sem=recv_sem,
                device_id=device, device_id_type=MESH,
            ).start()

    key_rows = pl.ds(pl.multiple_of(WINDOW + me_h * BLOCK, BLOCK), BLOCK)

    def send_kv(i, carry):
        device, head = target(i)
        is_self = jnp.logical_and(mine, i == 0)
        cols = pl.ds(pl.multiple_of(head * HEAD_WIDTH, HEAD_WIDTH), HEAD_WIDTH)
        send(is_self, device, k_ref.at[:, cols], kv.at[0, key_rows, :], s_k, r_kv.at[me_h])
        send(is_self, device, v_ref.at[:, cols], kv.at[1, key_rows, :], s_v, r_kv.at[me_h])
        return carry

    def send_qg(i, carry):
        device, head = target(i)
        is_self = jnp.logical_and(mine, i == 0)
        cols = pl.ds(pl.multiple_of(head * 2 * HEAD_WIDTH, 2 * HEAD_WIDTH), 2 * HEAD_WIDTH)
        send(is_self, device, q_ref.at[:, cols], qg.at[me_h, 0], s_q, r_qg.at[me_h])
        send(is_self, device, g_ref.at[:, cols], qg.at[me_h, 1], s_g, r_qg.at[me_h])
        return carry

    lax.fori_loop(0, n_blocks, send_kv, 0)
    lax.fori_loop(0, n_blocks, send_qg, 0)

    dk[...] = jnp.zeros_like(dk)
    dv[...] = jnp.zeros_like(dv)

    def take_kv(i, carry):
        h = source(i)
        rows = pl.ds(pl.multiple_of(WINDOW + h * BLOCK, BLOCK), BLOCK)
        bytes_of(kv.at[:, rows, :], r_kv.at[h]).wait()

        @pl.when(h >= half)
        def _():
            lead = pl.ds(pl.multiple_of((h - half) * BLOCK, BLOCK), BLOCK)
            pltpu.make_async_remote_copy(
                src_ref=kv.at[:, rows, :], dst_ref=kv.at[:, lead, :], send_sem=s_halo,
                recv_sem=r_halo, device_id=after, device_id_type=MESH,
            ).start()

        return carry

    lax.fori_loop(0, n_blocks, take_kv, 0)
    rows_mask.wait()
    bytes_of(kv.at[:, pl.ds(0, WINDOW), :], r_halo).wait()

    head_cols = pl.ds(pl.multiple_of(my_head * HEAD_WIDTH, HEAD_WIDTH), HEAD_WIDTH)
    pair_cols = pl.ds(pl.multiple_of(my_head * 2 * HEAD_WIDTH, 2 * HEAD_WIDTH), 2 * HEAD_WIDTH)

    def work(i, carry):
        h = source(i)
        bytes_of(qg.at[h], r_qg.at[h]).wait()
        bits = [
            (bits_ref[h, SPAN_BLOCKS - 1 - o] > 0) & (seg * n_blocks + h + o >= SPAN_BLOCKS - 1)
            for o in range(SPAN_BLOCKS)
        ]
        q2 = jnp.concatenate([qg[h, 0, :, :HEAD_WIDTH], qg[h, 0, :, HEAD_WIDTH:]], axis=0)
        g2 = jnp.concatenate([qg[h, 1, :, :HEAD_WIDTH], qg[h, 1, :, HEAD_WIDTH:]], axis=0)
        dq = block_grads(bits, h * BLOCK, q2, g2, kv, st, dp, pbs, dss, dk, dv)
        dqs[h] = jnp.concatenate([dq[:BLOCK], dq[BLOCK:]], axis=1).astype(BF16)
        is_self = jnp.logical_and(mine, h == me_h)
        send(is_self, (seg, h), dqs.at[h], dq_out.at[:, pair_cols], s_dq, r_dq)
        return carry

    lax.fori_loop(0, n_blocks, work, 0)

    halo_out[0] = (dk[pl.ds(0, WINDOW), :] * PRE_SCALE).astype(BF16)
    halo_out[1] = dv[pl.ds(0, WINDOW), :].astype(BF16)
    back = pltpu.make_async_remote_copy(
        src_ref=halo_out, dst_ref=halo_in, send_sem=s_back, recv_sem=r_back,
        device_id=before, device_id_type=MESH,
    )
    back.start()

    def send_dkv(h):
        is_self = jnp.logical_and(mine, h == me_h)
        send(is_self, (seg, h), dkvs.at[0, h], dk_out.at[:, head_cols], s_dk, r_dk)
        send(is_self, (seg, h), dkvs.at[1, h], dv_out.at[:, head_cols], s_dv, r_dv)

    def finish_low(h, carry):
        rows = pl.ds(pl.multiple_of(WINDOW + h * BLOCK, BLOCK), BLOCK)
        dkvs[0, h] = (dk[rows, :] * PRE_SCALE).astype(BF16)
        dkvs[1, h] = dv[rows, :].astype(BF16)
        send_dkv(h)
        return carry

    lax.fori_loop(0, half, finish_low, 0)
    back.wait_recv()

    def finish_high(h, carry):
        rows = pl.ds(pl.multiple_of(WINDOW + h * BLOCK, BLOCK), BLOCK)
        lead = pl.ds(pl.multiple_of((h - half) * BLOCK, BLOCK), BLOCK)
        dkvs[0, h] = (dk[rows, :] * PRE_SCALE + halo_in[0, lead, :].astype(F32)).astype(BF16)
        dkvs[1, h] = (dv[rows, :] + halo_in[1, lead, :].astype(F32)).astype(BF16)
        send_dkv(h)
        return carry

    lax.fori_loop(half, n_blocks, finish_high, 0)

    back.wait_send()
    bytes_of(kv.at[:, pl.ds(0, WINDOW), :], s_halo).wait()

    def sent(ref, width, sem):
        @pl.when(mine)
        def _():
            bytes_of(ref.at[:, pl.ds(0, (n_blocks - 1) * width)], sem).wait()

        @pl.when(jnp.logical_not(mine))
        def _():
            bytes_of(ref, sem).wait()

    for ref, width, sem in (
        (q_ref, 2 * HEAD_WIDTH, s_q),
        (g_ref, 2 * HEAD_WIDTH, s_g),
        (k_ref, HEAD_WIDTH, s_k),
        (v_ref, HEAD_WIDTH, s_v),
        (dq_out, 2 * HEAD_WIDTH, s_dq),
        (dk_out, HEAD_WIDTH, s_dk),
        (dv_out, HEAD_WIDTH, s_dv),
    ):
        sent(ref, width, sem)
    bytes_of(dq_out, r_dq).wait()
    bytes_of(dk_out, r_dk).wait()
    bytes_of(dv_out, r_dv).wait()


def solution(mesh):
    n_z = mesh.shape["ctx"] // 2
    n_blocks = mesh.shape["head"]

    def on_device(query, key, value, out_grad, block_mask):
        any_space = pl.BlockSpec(memory_space=pl.ANY)
        dma = pltpu.SemaphoreType.DMA
        keys = n_blocks * BLOCK + WINDOW
        cols = 2 * BLOCK

        def body(*refs):
            kernel(n_z, *refs)

        return pl.pallas_call(
            body,
            out_shape=(
                jax.ShapeDtypeStruct(query.shape, BF16),
                jax.ShapeDtypeStruct(key.shape, BF16),
                jax.ShapeDtypeStruct(value.shape, BF16),
            ),
            in_specs=[any_space] * 5,
            out_specs=(any_space,) * 3,
            scratch_shapes=[
                pltpu.VMEM((2, keys, HEAD_WIDTH), BF16),
                pltpu.VMEM((n_blocks, 2, BLOCK, 2 * HEAD_WIDTH), BF16),
                pltpu.VMEM((n_blocks, BLOCK, 2 * HEAD_WIDTH), BF16),
                pltpu.VMEM((2, n_blocks, BLOCK, HEAD_WIDTH), BF16),
                pltpu.VMEM((2, WINDOW, HEAD_WIDTH), BF16),
                pltpu.VMEM((2, WINDOW, HEAD_WIDTH), BF16),
                pltpu.VMEM((keys, HEAD_WIDTH), F32),
                pltpu.VMEM((keys, HEAD_WIDTH), F32),
                pltpu.VMEM((SPAN_BLOCKS, BLOCK, cols), F32),
                pltpu.VMEM((SPAN_BLOCKS, BLOCK, cols), F32),
                pltpu.VMEM((SPAN_BLOCKS * BLOCK, cols), BF16),
                pltpu.VMEM((SPAN_BLOCKS * BLOCK, cols), BF16),
                pltpu.SMEM((n_blocks, block_mask.shape[1]), jnp.int32),
                dma, dma, dma, dma, dma((n_blocks,)), dma((n_blocks,)),
                dma, dma, dma, dma, dma, dma, dma, dma, dma, dma, dma,
            ],
            compiler_params=pltpu.CompilerParams(collective_id=0, has_side_effects=True),
            name="window_attention_grads",
        )(query, key, value, out_grad, block_mask)

    tokens = P(("ctx", "head"), None)
    return jax.shard_map(
        on_device,
        mesh=mesh,
        in_specs=(tokens, tokens, tokens, tokens, P()),
        out_specs=(tokens, tokens, tokens),
        check_vma=False,
    )
```

```python
import math

import jax
import jax.numpy as jnp
from jax import lax
from jax.experimental import pallas as pl
from jax.experimental.pallas import tpu as pltpu
from jax.sharding import PartitionSpec as P

HEAD_WIDTH = 128
BLOCK = 128
LANES = 128
SPAN_BLOCKS = 9
CHUNK = 3
WINDOW = 1024
PRE_SCALE = 168.0 ** (-0.5)
EXP2_SCALE = PRE_SCALE / math.log(2.0)

F32 = jnp.float32
BF16 = jnp.bfloat16
MESH = pl.DeviceIdType.MESH

NT = (((1,), (1,)), ((), ()))
TN = (((0,), (0,)), ((), ()))
NN = (((1,), (0,)), ((), ()))


def dot(a, b, dims):
    return lax.dot_general(a, b, dims, preferred_element_type=F32)


def fold(x, op):
    return op(x.reshape(BLOCK // 8, 8, x.shape[1]), axis=0)


def bytes_of(ref, sem):
    return pltpu.make_async_copy(ref, ref, sem)


def block_grads(bits, first_row, q2, g2, kv, st, dp, pbs, dss, dk, dv):
    cols = q2.shape[0]
    u_index = lax.broadcasted_iota(jnp.int32, (BLOCK, cols), 0)
    t_index = lax.rem(lax.broadcasted_iota(jnp.int32, (BLOCK, cols), 1), BLOCK)
    causal = u_index <= t_index
    rows = CHUNK * BLOCK

    def span(c):
        return pl.ds(pl.multiple_of(first_row + c * rows, BLOCK), rows)

    m8 = jnp.full((8, cols), -jnp.inf, F32)
    for c in range(SPAN_BLOCKS // CHUNK):
        s = dot(kv[0, span(c), :], q2, NT)
        for i in range(CHUNK):
            o = c * CHUNK + i
            part = s[i * BLOCK : (i + 1) * BLOCK]
            if o == SPAN_BLOCKS - 1:
                part = jnp.where(causal, part, -jnp.inf)
            if o == 0:
                part = jnp.where(causal, -jnp.inf, part)
            st[o] = part
            m8 = jnp.maximum(m8, jnp.where(bits[o], fold(part, jnp.max), -jnp.inf))
    row_max = jnp.max(m8, axis=0, keepdims=True)

    l8 = jnp.zeros((8, cols), F32)
    d8 = jnp.zeros((8, cols), F32)
    for c in range(SPAN_BLOCKS // CHUNK):
        d = dot(kv[1, span(c), :], g2, NT)
        for i in range(CHUNK):
            o = c * CHUNK + i
            part = d[i * BLOCK : (i + 1) * BLOCK]
            shift = jnp.where(bits[o], row_max, jnp.inf)
            e = jnp.exp2((st[o] - shift) * EXP2_SCALE)
            st[o] = e
            dp[o] = part
            l8 += fold(e, jnp.sum)
            d8 += fold(e * part, jnp.sum)
    inverse = 1.0 / jnp.sum(l8, axis=0, keepdims=True)
    delta = jnp.sum(d8, axis=0, keepdims=True) * inverse

    dq = jnp.zeros((cols, HEAD_WIDTH), F32)
    for c in range(SPAN_BLOCKS // CHUNK):
        for i in range(CHUNK):
            o = c * CHUNK + i
            p = st[o] * inverse
            pbs[pl.ds(o * BLOCK, BLOCK), :] = p.astype(BF16)
            dss[pl.ds(o * BLOCK, BLOCK), :] = (p * (dp[o] - delta)).astype(BF16)
        pb = pbs[pl.ds(c * rows, rows), :]
        ds = dss[pl.ds(c * rows, rows), :]
        dv[span(c), :] += dot(pb, g2, NN)
        dk[span(c), :] += dot(ds, q2, NN)
        dq += dot(ds, kv[0, span(c), :], TN)
    return dq * PRE_SCALE


def kernel(
    n_z, q_ref, k_ref, v_ref, g_ref, mask_ref, dq_out, dk_out, dv_out,
    kv, qg, dqs, dkvs, halo_out, halo_in, dk, dv, st, dp, pbs, dss, bits_ref,
    s_q, s_g, s_k, s_v, r_qg, r_kv, s_halo, r_halo, s_back, r_back,
    s_dq, s_dk, s_dv, r_dq, r_dk, r_dv, m_sem,
):
    ctx = lax.axis_index("ctx")
    me_h = lax.axis_index("head")
    z, xh = lax.div(ctx, 2), lax.rem(ctx, 2)
    y, xl, core = lax.div(me_h, 4), lax.rem(lax.div(me_h, 2), 2), lax.rem(me_h, 2)
    x = xh * 2 + xl
    my_head = x * 4 + y
    seg = z * 2 + core
    n_blocks = qg.shape[0]
    half = n_blocks // 2
    other = me_h + 1 - 2 * core
    after = (lax.rem(z + core, n_z) * 2 + xh, other)
    before = (lax.rem(z + n_z - 1 + core, n_z) * 2 + xh, other)

    way = 1 - 2 * core

    def pair_step(pair):
        dx = lax.rem(pair, 2)
        return dx, lax.rem(lax.div(pair, 2) + 2 * dx, 4)

    def target(i):
        pair, second = lax.div(i, 2), lax.rem(i, 2)
        dx, dy = pair_step(pair)
        dx = dx + 2 * second
        tx, ty = lax.rem(x + 4 + way * dx, 4), lax.rem(y + 4 + way * dy, 4)
        return (z * 2 + lax.div(tx, 2), ty * 4 + lax.rem(tx, 2) * 2 + xh), tx * 4 + ty

    def source(i):
        pair, sc = lax.div(i, 2), lax.rem(i, 2)
        dx, dy = pair_step(pair)
        return lax.rem(y + 4 - (1 - 2 * sc) * dy, 4) * 4 + lax.rem(x + dx, 2) * 2 + sc

    lanes = bits_ref.shape[1]
    seg_lane = lax.rem(seg * n_blocks, lanes)
    lane_tile = pl.ds(pl.multiple_of(lax.div(seg * n_blocks, lanes) * lanes, lanes), lanes)
    rows_mask = pltpu.make_async_copy(mask_ref.at[:, lane_tile], bits_ref, m_sem)
    rows_mask.start()

    barrier = pltpu.get_barrier_semaphore()

    def greet(i, carry):
        device, _ = target(i)
        pl.semaphore_signal(barrier, inc=1, device_id=device, device_id_type=MESH)
        pl.semaphore_signal(barrier, inc=1, device_id=(seg, i), device_id_type=MESH)
        return carry

    lax.fori_loop(0, n_blocks, greet, 0)
    pl.semaphore_signal(barrier, inc=1, device_id=after, device_id_type=MESH)
    pl.semaphore_signal(barrier, inc=1, device_id=before, device_id_type=MESH)
    pl.semaphore_wait(barrier, 2 * n_blocks + 2)

    mine = xh == core

    def send(is_self, device, src, dst, send_sem, recv_sem):
        @pl.when(is_self)
        def _():
            pltpu.make_async_copy(src, dst, recv_sem).start()

        @pl.when(jnp.logical_not(is_self))
        def _():
            pltpu.make_async_remote_copy(
                src_ref=src, dst_ref=dst, send_sem=send_sem, recv_sem=recv_sem,
                device_id=device, device_id_type=MESH,
            ).start()

    key_rows = pl.ds(pl.multiple_of(WINDOW + me_h * BLOCK, BLOCK), BLOCK)

    def send_kv(i, carry):
        device, head = target(i)
        is_self = jnp.logical_and(mine, head == my_head)
        cols = pl.ds(pl.multiple_of(head * HEAD_WIDTH, HEAD_WIDTH), HEAD_WIDTH)
        send(is_self, device, k_ref.at[:, cols], kv.at[0, key_rows, :], s_k, r_kv.at[me_h])
        send(is_self, device, v_ref.at[:, cols], kv.at[1, key_rows, :], s_v, r_kv.at[me_h])
        return carry

    def send_qg(i, carry):
        device, head = target(i)
        is_self = jnp.logical_and(mine, head == my_head)
        cols = pl.ds(pl.multiple_of(head * 2 * HEAD_WIDTH, 2 * HEAD_WIDTH), 2 * HEAD_WIDTH)
        send(is_self, device, q_ref.at[:, cols], qg.at[me_h, 0], s_q, r_qg.at[me_h])
        send(is_self, device, g_ref.at[:, cols], qg.at[me_h, 1], s_g, r_qg.at[me_h])
        return carry

    lax.fori_loop(0, n_blocks, send_kv, 0)
    lax.fori_loop(0, n_blocks, send_qg, 0)

    dk[...] = jnp.zeros_like(dk)
    dv[...] = jnp.zeros_like(dv)

    def take_kv(i, carry):
        h = source(i)
        rows = pl.ds(pl.multiple_of(WINDOW + h * BLOCK, BLOCK), BLOCK)
        bytes_of(kv.at[:, rows, :], r_kv.at[h]).wait()

        @pl.when(h >= half)
        def _():
            lead = pl.ds(pl.multiple_of((h - half) * BLOCK, BLOCK), BLOCK)
            pltpu.make_async_remote_copy(
                src_ref=kv.at[:, rows, :], dst_ref=kv.at[:, lead, :], send_sem=s_halo,
                recv_sem=r_halo, device_id=after, device_id_type=MESH,
            ).start()

        return carry

    lax.fori_loop(0, n_blocks, take_kv, 0)
    rows_mask.wait()
    bytes_of(kv.at[:, pl.ds(0, WINDOW), :], r_halo).wait()

    head_cols = pl.ds(pl.multiple_of(my_head * HEAD_WIDTH, HEAD_WIDTH), HEAD_WIDTH)
    pair_cols = pl.ds(pl.multiple_of(my_head * 2 * HEAD_WIDTH, 2 * HEAD_WIDTH), 2 * HEAD_WIDTH)

    def work(i, carry):
        h = source(i)
        bytes_of(qg.at[h], r_qg.at[h]).wait()
        bits = [
            (bits_ref[SPAN_BLOCKS - 1 - o, seg_lane + h] > 0) & (seg * n_blocks + h + o >= SPAN_BLOCKS - 1)
            for o in range(SPAN_BLOCKS)
        ]
        q2 = jnp.concatenate([qg[h, 0, :, :HEAD_WIDTH], qg[h, 0, :, HEAD_WIDTH:]], axis=0)
        g2 = jnp.concatenate([qg[h, 1, :, :HEAD_WIDTH], qg[h, 1, :, HEAD_WIDTH:]], axis=0)
        dq = block_grads(bits, h * BLOCK, q2, g2, kv, st, dp, pbs, dss, dk, dv)
        dqs[h] = jnp.concatenate([dq[:BLOCK], dq[BLOCK:]], axis=1).astype(BF16)
        is_self = jnp.logical_and(mine, h == me_h)
        send(is_self, (seg, h), dqs.at[h], dq_out.at[:, pair_cols], s_dq, r_dq)
        return carry

    lax.fori_loop(0, n_blocks, work, 0)

    halo_out[0] = (dk[pl.ds(0, WINDOW), :] * PRE_SCALE).astype(BF16)
    halo_out[1] = dv[pl.ds(0, WINDOW), :].astype(BF16)
    back = pltpu.make_async_remote_copy(
        src_ref=halo_out, dst_ref=halo_in, send_sem=s_back, recv_sem=r_back,
        device_id=before, device_id_type=MESH,
    )
    back.start()

    def send_dkv(h):
        is_self = jnp.logical_and(mine, h == me_h)
        send(is_self, (seg, h), dkvs.at[0, h], dk_out.at[:, head_cols], s_dk, r_dk)
        send(is_self, (seg, h), dkvs.at[1, h], dv_out.at[:, head_cols], s_dv, r_dv)

    def finish_low(h, carry):
        rows = pl.ds(pl.multiple_of(WINDOW + h * BLOCK, BLOCK), BLOCK)
        dkvs[0, h] = (dk[rows, :] * PRE_SCALE).astype(BF16)
        dkvs[1, h] = dv[rows, :].astype(BF16)
        send_dkv(h)
        return carry

    lax.fori_loop(0, half, finish_low, 0)
    back.wait_recv()

    def finish_high(h, carry):
        rows = pl.ds(pl.multiple_of(WINDOW + h * BLOCK, BLOCK), BLOCK)
        lead = pl.ds(pl.multiple_of((h - half) * BLOCK, BLOCK), BLOCK)
        dkvs[0, h] = (dk[rows, :] * PRE_SCALE + halo_in[0, lead, :].astype(F32)).astype(BF16)
        dkvs[1, h] = (dv[rows, :] + halo_in[1, lead, :].astype(F32)).astype(BF16)
        send_dkv(h)
        return carry

    lax.fori_loop(half, n_blocks, finish_high, 0)

    back.wait_send()
    bytes_of(kv.at[:, pl.ds(0, WINDOW), :], s_halo).wait()

    def sent(ref, width, sem):
        @pl.when(mine)
        def _():
            bytes_of(ref.at[:, pl.ds(0, (n_blocks - 1) * width)], sem).wait()

        @pl.when(jnp.logical_not(mine))
        def _():
            bytes_of(ref, sem).wait()

    for ref, width, sem in (
        (q_ref, 2 * HEAD_WIDTH, s_q),
        (g_ref, 2 * HEAD_WIDTH, s_g),
        (k_ref, HEAD_WIDTH, s_k),
        (v_ref, HEAD_WIDTH, s_v),
        (dq_out, 2 * HEAD_WIDTH, s_dq),
        (dk_out, HEAD_WIDTH, s_dk),
        (dv_out, HEAD_WIDTH, s_dv),
    ):
        sent(ref, width, sem)
    bytes_of(dq_out, r_dq).wait()
    bytes_of(dk_out, r_dk).wait()
    bytes_of(dv_out, r_dv).wait()


def put_out(a, b, c, a_out, b_out, c_out, a_sem, b_sem, c_sem):
    copies = [
        pltpu.make_async_copy(src, dst, sem)
        for src, dst, sem in ((a, a_out, a_sem), (b, b_out, b_sem), (c, c_out, c_sem))
    ]
    for copy in copies:
        copy.start()
    for copy in copies:
        copy.wait()


def solution(mesh):
    n_z = mesh.shape["ctx"] // 2
    n_blocks = mesh.shape["head"]

    def on_device(query, key, value, out_grad, block_mask):
        any_space = pl.BlockSpec(memory_space=pl.ANY)
        dma = pltpu.SemaphoreType.DMA
        keys = n_blocks * BLOCK + WINDOW
        cols = 2 * BLOCK

        def body(*refs):
            kernel(n_z, *refs)

        landed = pl.pallas_call(
            body,
            out_shape=(
                jax.ShapeDtypeStruct(query.shape, BF16),
                jax.ShapeDtypeStruct(key.shape, BF16),
                jax.ShapeDtypeStruct(value.shape, BF16),
            ),
            in_specs=[any_space] * 5,
            out_specs=(any_space,) * 3,
            scratch_shapes=[
                pltpu.VMEM((2, keys, HEAD_WIDTH), BF16),
                pltpu.VMEM((n_blocks, 2, BLOCK, 2 * HEAD_WIDTH), BF16),
                pltpu.VMEM((n_blocks, BLOCK, 2 * HEAD_WIDTH), BF16),
                pltpu.VMEM((2, n_blocks, BLOCK, HEAD_WIDTH), BF16),
                pltpu.VMEM((2, WINDOW, HEAD_WIDTH), BF16),
                pltpu.VMEM((2, WINDOW, HEAD_WIDTH), BF16),
                pltpu.VMEM((keys, HEAD_WIDTH), F32),
                pltpu.VMEM((keys, HEAD_WIDTH), F32),
                pltpu.VMEM((SPAN_BLOCKS, BLOCK, cols), F32),
                pltpu.VMEM((SPAN_BLOCKS, BLOCK, cols), F32),
                pltpu.VMEM((SPAN_BLOCKS * BLOCK, cols), BF16),
                pltpu.VMEM((SPAN_BLOCKS * BLOCK, cols), BF16),
                pltpu.SMEM((block_mask.shape[1], LANES), jnp.int32),
                dma, dma, dma, dma, dma((n_blocks,)), dma((n_blocks,)),
                dma, dma, dma, dma, dma, dma, dma, dma, dma, dma, dma,
            ],
            compiler_params=pltpu.CompilerParams(collective_id=0, has_side_effects=True),
            name="window_attention_grads",
        )(query, key, value, out_grad, block_mask.T)
        return pl.pallas_call(
            put_out,
            out_shape=tuple(jax.ShapeDtypeStruct(a.shape, BF16) for a in (query, key, value)),
            in_specs=[pl.BlockSpec(memory_space=pltpu.VMEM)] * 3,
            out_specs=(any_space,) * 3,
            scratch_shapes=[dma, dma, dma],
            name="put_out",
        )(*landed)

    tokens = P(("ctx", "head"), None)
    return jax.shard_map(
        on_device,
        mesh=mesh,
        in_specs=(tokens, tokens, tokens, tokens, P()),
        out_specs=(tokens, tokens, tokens),
        check_vma=False,
    )
```

```python
import math

import jax
import jax.numpy as jnp
from jax import lax
from jax.experimental import pallas as pl
from jax.experimental.pallas import tpu as pltpu
from jax.sharding import PartitionSpec as P

HEAD_WIDTH = 128
BLOCK = 128
LANES = 128
SPAN_BLOCKS = 9
CHUNK = 3
WINDOW = 1024
PRE_SCALE = 168.0 ** (-0.5)
EXP2_SCALE = PRE_SCALE / math.log(2.0)

F32 = jnp.float32
BF16 = jnp.bfloat16
MESH = pl.DeviceIdType.MESH

NT = (((1,), (1,)), ((), ()))
TN = (((0,), (0,)), ((), ()))
NN = (((1,), (0,)), ((), ()))


def dot(a, b, dims):
    return lax.dot_general(a, b, dims, preferred_element_type=F32)


def fold(x, op):
    return op(x.reshape(BLOCK // 8, 8, x.shape[1]), axis=0)


def bytes_of(ref, sem):
    return pltpu.make_async_copy(ref, ref, sem)


def block_grads(bits, first_row, q2, g2, kv, st, dp, pbs, dss, dk, dv):
    cols = q2.shape[0]
    u_index = lax.broadcasted_iota(jnp.int32, (BLOCK, cols), 0)
    t_index = lax.rem(lax.broadcasted_iota(jnp.int32, (BLOCK, cols), 1), BLOCK)
    causal = u_index <= t_index
    rows = CHUNK * BLOCK

    def span(c):
        return pl.ds(pl.multiple_of(first_row + c * rows, BLOCK), rows)

    m8 = jnp.full((8, cols), -jnp.inf, F32)
    for c in range(SPAN_BLOCKS // CHUNK):
        s = dot(kv[0, span(c), :], q2, NT)
        for i in range(CHUNK):
            o = c * CHUNK + i
            part = s[i * BLOCK : (i + 1) * BLOCK]
            if o == SPAN_BLOCKS - 1:
                part = jnp.where(causal, part, -jnp.inf)
            if o == 0:
                part = jnp.where(causal, -jnp.inf, part)
            st[o] = part
            m8 = jnp.maximum(m8, jnp.where(bits[o], fold(part, jnp.max), -jnp.inf))
    row_max = jnp.max(m8, axis=0, keepdims=True)

    l8 = jnp.zeros((8, cols), F32)
    d8 = jnp.zeros((8, cols), F32)
    for c in range(SPAN_BLOCKS // CHUNK):
        d = dot(kv[1, span(c), :], g2, NT)
        for i in range(CHUNK):
            o = c * CHUNK + i
            part = d[i * BLOCK : (i + 1) * BLOCK]
            shift = jnp.where(bits[o], row_max, jnp.inf)
            e = jnp.exp2((st[o] - shift) * EXP2_SCALE)
            st[o] = e
            dp[o] = part
            l8 += fold(e, jnp.sum)
            d8 += fold(e * part, jnp.sum)
    inverse = 1.0 / jnp.sum(l8, axis=0, keepdims=True)
    delta = jnp.sum(d8, axis=0, keepdims=True) * inverse

    dq = jnp.zeros((cols, HEAD_WIDTH), F32)
    for c in range(SPAN_BLOCKS // CHUNK):
        for i in range(CHUNK):
            o = c * CHUNK + i
            p = st[o] * inverse
            pbs[pl.ds(o * BLOCK, BLOCK), :] = p.astype(BF16)
            dss[pl.ds(o * BLOCK, BLOCK), :] = (p * (dp[o] - delta)).astype(BF16)
        pb = pbs[pl.ds(c * rows, rows), :]
        ds = dss[pl.ds(c * rows, rows), :]
        dv[span(c), :] += dot(pb, g2, NN)
        dk[span(c), :] += dot(ds, q2, NN)
        dq += dot(ds, kv[0, span(c), :], TN)
    return dq * PRE_SCALE


def kernel(
    n_z, q_ref, k_ref, v_ref, g_ref, mask_ref, dq_out, dk_out, dv_out,
    kv, qg, dqs, dkvs, halo_out, halo_in, dk, dv, st, dp, pbs, dss, bits_ref,
    s_q, s_g, s_k, s_v, r_qg, r_kv, s_halo, r_halo, s_back, r_back,
    s_dq, s_dk, s_dv, r_dq, r_dk, r_dv, m_sem,
):
    ctx = lax.axis_index("ctx")
    me_h = lax.axis_index("head")
    z, xh = lax.div(ctx, 2), lax.rem(ctx, 2)
    y, xl, core = lax.div(me_h, 4), lax.rem(lax.div(me_h, 2), 2), lax.rem(me_h, 2)
    x = xh * 2 + xl
    my_head = x * 4 + y
    seg = z * 2 + core
    n_blocks = qg.shape[0]
    half = n_blocks // 2
    other = me_h + 1 - 2 * core
    after = (lax.rem(z + core, n_z) * 2 + xh, other)
    before = (lax.rem(z + n_z - 1 + core, n_z) * 2 + xh, other)

    way = 1 - 2 * core

    def pair_step(pair):
        dx = lax.rem(pair, 2)
        return dx, lax.rem(lax.div(pair, 2) + 2 * dx, 4)

    def target(i):
        pair, second = lax.div(i, 2), lax.rem(i, 2)
        dx, dy = pair_step(pair)
        dx = dx + 2 * second
        tx, ty = lax.rem(x + 4 + way * dx, 4), lax.rem(y + 4 + way * dy, 4)
        return (z * 2 + lax.div(tx, 2), ty * 4 + lax.rem(tx, 2) * 2 + xh), tx * 4 + ty

    def source(i):
        pair, sc = lax.div(i, 2), lax.rem(i, 2)
        dx, dy = pair_step(pair)
        return lax.rem(y + 4 - (1 - 2 * sc) * dy, 4) * 4 + lax.rem(x + dx, 2) * 2 + sc

    lanes = bits_ref.shape[1]
    seg_lane = lax.rem(seg * n_blocks, lanes)
    lane_tile = pl.ds(pl.multiple_of(lax.div(seg * n_blocks, lanes) * lanes, lanes), lanes)
    rows_mask = pltpu.make_async_copy(mask_ref.at[:, lane_tile], bits_ref, m_sem)
    rows_mask.start()

    barrier = pltpu.get_barrier_semaphore()

    def greet(i, carry):
        device, _ = target(i)
        pl.semaphore_signal(barrier, inc=1, device_id=device, device_id_type=MESH)
        pl.semaphore_signal(barrier, inc=1, device_id=(seg, i), device_id_type=MESH)
        return carry

    lax.fori_loop(0, n_blocks, greet, 0)
    pl.semaphore_signal(barrier, inc=1, device_id=after, device_id_type=MESH)
    pl.semaphore_signal(barrier, inc=1, device_id=before, device_id_type=MESH)
    pl.semaphore_wait(barrier, 2 * n_blocks + 2)

    mine = xh == core

    def send(is_self, device, src, dst, send_sem, recv_sem):
        @pl.when(is_self)
        def _():
            pltpu.make_async_copy(src, dst, recv_sem).start()

        @pl.when(jnp.logical_not(is_self))
        def _():
            pltpu.make_async_remote_copy(
                src_ref=src, dst_ref=dst, send_sem=send_sem, recv_sem=recv_sem,
                device_id=device, device_id_type=MESH,
            ).start()

    key_rows = pl.ds(pl.multiple_of(WINDOW + me_h * BLOCK, BLOCK), BLOCK)

    def send_kv(i, carry):
        device, head = target(i)
        is_self = jnp.logical_and(mine, head == my_head)
        cols = pl.ds(pl.multiple_of(head * HEAD_WIDTH, HEAD_WIDTH), HEAD_WIDTH)
        send(is_self, device, k_ref.at[:, cols], kv.at[0, key_rows, :], s_k, r_kv.at[me_h])
        send(is_self, device, v_ref.at[:, cols], kv.at[1, key_rows, :], s_v, r_kv.at[me_h])
        return carry

    def send_qg(i, carry):
        device, head = target(i)
        is_self = jnp.logical_and(mine, head == my_head)
        cols = pl.ds(pl.multiple_of(head * 2 * HEAD_WIDTH, 2 * HEAD_WIDTH), 2 * HEAD_WIDTH)
        send(is_self, device, q_ref.at[:, cols], qg.at[me_h, 0], s_q, r_qg.at[me_h])
        send(is_self, device, g_ref.at[:, cols], qg.at[me_h, 1], s_g, r_qg.at[me_h])
        return carry

    lax.fori_loop(0, n_blocks, send_kv, 0)
    lax.fori_loop(0, n_blocks, send_qg, 0)

    dk[...] = jnp.zeros_like(dk)
    dv[...] = jnp.zeros_like(dv)

    def take_kv(i, carry):
        h = source(i)
        rows = pl.ds(pl.multiple_of(WINDOW + h * BLOCK, BLOCK), BLOCK)
        bytes_of(kv.at[:, rows, :], r_kv.at[h]).wait()

        @pl.when(h >= half)
        def _():
            lead = pl.ds(pl.multiple_of((h - half) * BLOCK, BLOCK), BLOCK)
            pltpu.make_async_remote_copy(
                src_ref=kv.at[:, rows, :], dst_ref=kv.at[:, lead, :], send_sem=s_halo,
                recv_sem=r_halo, device_id=after, device_id_type=MESH,
            ).start()

        return carry

    lax.fori_loop(0, n_blocks, take_kv, 0)
    rows_mask.wait()
    bytes_of(kv.at[:, pl.ds(0, WINDOW), :], r_halo).wait()

    head_cols = pl.ds(pl.multiple_of(my_head * HEAD_WIDTH, HEAD_WIDTH), HEAD_WIDTH)
    pair_cols = pl.ds(pl.multiple_of(my_head * 2 * HEAD_WIDTH, 2 * HEAD_WIDTH), 2 * HEAD_WIDTH)

    def work(i, carry):
        h = source(i)
        bytes_of(qg.at[h], r_qg.at[h]).wait()
        bits = [
            (bits_ref[SPAN_BLOCKS - 1 - o, seg_lane + h] > 0) & (seg * n_blocks + h + o >= SPAN_BLOCKS - 1)
            for o in range(SPAN_BLOCKS)
        ]
        q2 = jnp.concatenate([qg[h, 0, :, :HEAD_WIDTH], qg[h, 0, :, HEAD_WIDTH:]], axis=0)
        g2 = jnp.concatenate([qg[h, 1, :, :HEAD_WIDTH], qg[h, 1, :, HEAD_WIDTH:]], axis=0)
        dq = block_grads(bits, h * BLOCK, q2, g2, kv, st, dp, pbs, dss, dk, dv)
        dqs[h] = jnp.concatenate([dq[:BLOCK], dq[BLOCK:]], axis=1).astype(BF16)
        is_self = jnp.logical_and(mine, h == me_h)
        send(is_self, (seg, h), dqs.at[h], dq_out.at[:, pair_cols], s_dq, r_dq)
        return carry

    lax.fori_loop(0, n_blocks, work, 0)

    halo_out[0] = (dk[pl.ds(0, WINDOW), :] * PRE_SCALE).astype(BF16)
    halo_out[1] = dv[pl.ds(0, WINDOW), :].astype(BF16)
    back = pltpu.make_async_remote_copy(
        src_ref=halo_out, dst_ref=halo_in, send_sem=s_back, recv_sem=r_back,
        device_id=before, device_id_type=MESH,
    )
    back.start()

    def send_dkv(h):
        is_self = jnp.logical_and(mine, h == me_h)
        send(is_self, (seg, h), dkvs.at[0, h], dk_out.at[:, head_cols], s_dk, r_dk)
        send(is_self, (seg, h), dkvs.at[1, h], dv_out.at[:, head_cols], s_dv, r_dv)

    def finish_low(h, carry):
        rows = pl.ds(pl.multiple_of(WINDOW + h * BLOCK, BLOCK), BLOCK)
        dkvs[0, h] = (dk[rows, :] * PRE_SCALE).astype(BF16)
        dkvs[1, h] = dv[rows, :].astype(BF16)
        send_dkv(h)
        return carry

    lax.fori_loop(0, half, finish_low, 0)
    back.wait_recv()

    def finish_high(h, carry):
        rows = pl.ds(pl.multiple_of(WINDOW + h * BLOCK, BLOCK), BLOCK)
        lead = pl.ds(pl.multiple_of((h - half) * BLOCK, BLOCK), BLOCK)
        dkvs[0, h] = (dk[rows, :] * PRE_SCALE + halo_in[0, lead, :].astype(F32)).astype(BF16)
        dkvs[1, h] = (dv[rows, :] + halo_in[1, lead, :].astype(F32)).astype(BF16)
        send_dkv(h)
        return carry

    lax.fori_loop(half, n_blocks, finish_high, 0)

    back.wait_send()
    bytes_of(kv.at[:, pl.ds(0, WINDOW), :], s_halo).wait()

    def sent(ref, width, sem):
        @pl.when(mine)
        def _():
            bytes_of(ref.at[:, pl.ds(0, (n_blocks - 1) * width)], sem).wait()

        @pl.when(jnp.logical_not(mine))
        def _():
            bytes_of(ref, sem).wait()

    for ref, width, sem in (
        (q_ref, 2 * HEAD_WIDTH, s_q),
        (g_ref, 2 * HEAD_WIDTH, s_g),
        (k_ref, HEAD_WIDTH, s_k),
        (v_ref, HEAD_WIDTH, s_v),
        (dq_out, 2 * HEAD_WIDTH, s_dq),
        (dk_out, HEAD_WIDTH, s_dk),
        (dv_out, HEAD_WIDTH, s_dv),
    ):
        sent(ref, width, sem)
    bytes_of(dq_out, r_dq).wait()
    bytes_of(dk_out, r_dk).wait()
    bytes_of(dv_out, r_dv).wait()


def put_out(a, b, c, a_out, b_out, c_out, a_sem, b_sem, c_sem):
    copies = [
        pltpu.make_async_copy(src, dst, sem)
        for src, dst, sem in ((a, a_out, a_sem), (b, b_out, b_sem), (c, c_out, c_sem))
    ]
    for copy in copies:
        copy.start()
    for copy in copies:
        copy.wait()


def solution(mesh):
    n_z = mesh.shape["ctx"] // 2
    n_blocks = mesh.shape["head"]

    def on_device(query, key, value, out_grad, block_mask):
        any_space = pl.BlockSpec(memory_space=pl.ANY)
        dma = pltpu.SemaphoreType.DMA
        keys = n_blocks * BLOCK + WINDOW
        cols = 2 * BLOCK

        def body(*refs):
            kernel(n_z, *refs)

        landed = pl.pallas_call(
            body,
            out_shape=(
                pltpu.VMEM(query.shape, BF16),
                pltpu.VMEM(key.shape, BF16),
                pltpu.VMEM(value.shape, BF16),
            ),
            in_specs=[any_space] * 5,
            out_specs=(pl.BlockSpec(memory_space=pltpu.VMEM),) * 3,
            scratch_shapes=[
                pltpu.VMEM((2, keys, HEAD_WIDTH), BF16),
                pltpu.VMEM((n_blocks, 2, BLOCK, 2 * HEAD_WIDTH), BF16),
                pltpu.VMEM((n_blocks, BLOCK, 2 * HEAD_WIDTH), BF16),
                pltpu.VMEM((2, n_blocks, BLOCK, HEAD_WIDTH), BF16),
                pltpu.VMEM((2, WINDOW, HEAD_WIDTH), BF16),
                pltpu.VMEM((2, WINDOW, HEAD_WIDTH), BF16),
                pltpu.VMEM((keys, HEAD_WIDTH), F32),
                pltpu.VMEM((keys, HEAD_WIDTH), F32),
                pltpu.VMEM((SPAN_BLOCKS, BLOCK, cols), F32),
                pltpu.VMEM((SPAN_BLOCKS, BLOCK, cols), F32),
                pltpu.VMEM((SPAN_BLOCKS * BLOCK, cols), BF16),
                pltpu.VMEM((SPAN_BLOCKS * BLOCK, cols), BF16),
                pltpu.SMEM((block_mask.shape[1], LANES), jnp.int32),
                dma, dma, dma, dma, dma((n_blocks,)), dma((n_blocks,)),
                dma, dma, dma, dma, dma, dma, dma, dma, dma, dma, dma,
            ],
            compiler_params=pltpu.CompilerParams(collective_id=0, has_side_effects=True),
            name="window_attention_grads",
        )(query, key, value, out_grad, block_mask.T)
        return pl.pallas_call(
            put_out,
            out_shape=tuple(jax.ShapeDtypeStruct(a.shape, BF16) for a in (query, key, value)),
            in_specs=[any_space] * 3,
            out_specs=(any_space,) * 3,
            scratch_shapes=[dma, dma, dma],
            name="put_out",
            compiler_params=pltpu.CompilerParams(vmem_limit_bytes=2**20),
        )(*landed)

    tokens = P(("ctx", "head"), None)
    return jax.shard_map(
        on_device,
        mesh=mesh,
        in_specs=(tokens, tokens, tokens, tokens, P()),
        out_specs=(tokens, tokens, tokens),
        check_vma=False,
    )
```

```python
import math

import jax
import jax.numpy as jnp
from jax import lax
from jax.experimental import pallas as pl
from jax.experimental.pallas import tpu as pltpu
from jax.sharding import PartitionSpec as P

HEAD_WIDTH = 128
BLOCK = 128
LANES = 128
SPAN_BLOCKS = 9
CHUNK = 3
WINDOW = 1024
PRE_SCALE = 168.0 ** (-0.5)
EXP2_SCALE = PRE_SCALE / math.log(2.0)

F32 = jnp.float32
BF16 = jnp.bfloat16
MESH = pl.DeviceIdType.MESH

NT = (((1,), (1,)), ((), ()))
TN = (((0,), (0,)), ((), ()))
NN = (((1,), (0,)), ((), ()))


def dot(a, b, dims):
    return lax.dot_general(a, b, dims, preferred_element_type=F32)


def fold(x, op):
    return op(x.reshape(BLOCK // 8, 8, x.shape[1]), axis=0)


def bytes_of(ref, sem):
    return pltpu.make_async_copy(ref, ref, sem)


def block_grads(bits, first_row, q2, g2, kv, st, dp, pbs, dss, dk, dv):
    cols = q2.shape[0]
    u_index = lax.broadcasted_iota(jnp.int32, (BLOCK, cols), 0)
    t_index = lax.rem(lax.broadcasted_iota(jnp.int32, (BLOCK, cols), 1), BLOCK)
    causal = u_index <= t_index
    rows = CHUNK * BLOCK

    def span(c):
        return pl.ds(pl.multiple_of(first_row + c * rows, BLOCK), rows)

    m8 = jnp.full((8, cols), -jnp.inf, F32)
    for c in range(SPAN_BLOCKS // CHUNK):
        s = dot(kv[0, span(c), :], q2, NT)
        for i in range(CHUNK):
            o = c * CHUNK + i
            part = s[i * BLOCK : (i + 1) * BLOCK]
            if o == SPAN_BLOCKS - 1:
                part = jnp.where(causal, part, -jnp.inf)
            if o == 0:
                part = jnp.where(causal, -jnp.inf, part)
            st[o] = part
            m8 = jnp.maximum(m8, jnp.where(bits[o], fold(part, jnp.max), -jnp.inf))
    row_max = jnp.max(m8, axis=0, keepdims=True)

    l8 = jnp.zeros((8, cols), F32)
    d8 = jnp.zeros((8, cols), F32)
    for c in range(SPAN_BLOCKS // CHUNK):
        d = dot(kv[1, span(c), :], g2, NT)
        for i in range(CHUNK):
            o = c * CHUNK + i
            part = d[i * BLOCK : (i + 1) * BLOCK]
            shift = jnp.where(bits[o], row_max, jnp.inf)
            e = jnp.exp2((st[o] - shift) * EXP2_SCALE)
            st[o] = e
            dp[o] = part
            l8 += fold(e, jnp.sum)
            d8 += fold(e * part, jnp.sum)
    inverse = 1.0 / jnp.sum(l8, axis=0, keepdims=True)
    delta = jnp.sum(d8, axis=0, keepdims=True) * inverse

    dq = jnp.zeros((cols, HEAD_WIDTH), F32)
    for c in range(SPAN_BLOCKS // CHUNK):
        for i in range(CHUNK):
            o = c * CHUNK + i
            p = st[o] * inverse
            pbs[pl.ds(o * BLOCK, BLOCK), :] = p.astype(BF16)
            dss[pl.ds(o * BLOCK, BLOCK), :] = (p * (dp[o] - delta)).astype(BF16)
        pb = pbs[pl.ds(c * rows, rows), :]
        ds = dss[pl.ds(c * rows, rows), :]
        dv[span(c), :] += dot(pb, g2, NN)
        dk[span(c), :] += dot(ds, q2, NN)
        dq += dot(ds, kv[0, span(c), :], TN)
    return dq * PRE_SCALE


def kernel(
    n_z, q_ref, k_ref, v_ref, g_ref, mask_ref, dq_out, dk_out, dv_out,
    kv, qg, dqs, dkvs, halo_out, halo_in, dk, dv, st, dp, pbs, dss, bits_ref,
    s_q, s_g, s_k, s_v, r_qg, r_kv, s_halo, r_halo, s_back, r_back,
    s_dq, s_dk, s_dv, r_dq, r_dk, r_dv, m_sem, peer_sem,
):
    ctx = lax.axis_index("ctx")
    me_h = lax.axis_index("head")
    z, xh = lax.div(ctx, 2), lax.rem(ctx, 2)
    y, xl, core = lax.div(me_h, 4), lax.rem(lax.div(me_h, 2), 2), lax.rem(me_h, 2)
    x = xh * 2 + xl
    my_head = x * 4 + y
    seg = z * 2 + core
    n_blocks = qg.shape[0]
    half = n_blocks // 2
    other = me_h + 1 - 2 * core
    after = (lax.rem(z + core, n_z) * 2 + xh, other)
    before = (lax.rem(z + n_z - 1 + core, n_z) * 2 + xh, other)

    way = 1 - 2 * core

    def pair_step(pair):
        dx = lax.rem(pair, 2)
        return dx, lax.rem(lax.div(pair, 2) + 2 * dx, 4)

    def target(i):
        pair, second = lax.div(i, 2), lax.rem(i, 2)
        dx, dy = pair_step(pair)
        dx = dx + 2 * second
        tx, ty = lax.rem(x + 4 + way * dx, 4), lax.rem(y + 4 + way * dy, 4)
        return (z * 2 + lax.div(tx, 2), ty * 4 + lax.rem(tx, 2) * 2 + xh), tx * 4 + ty

    def source(i):
        pair, sc = lax.div(i, 2), lax.rem(i, 2)
        dx, dy = pair_step(pair)
        return lax.rem(y + 4 - (1 - 2 * sc) * dy, 4) * 4 + lax.rem(x + dx, 2) * 2 + sc

    lanes = bits_ref.shape[1]
    seg_lane = lax.rem(seg * n_blocks, lanes)
    lane_tile = pl.ds(pl.multiple_of(lax.div(seg * n_blocks, lanes) * lanes, lanes), lanes)
    rows_mask = pltpu.make_async_copy(mask_ref.at[:, lane_tile], bits_ref, m_sem)
    rows_mask.start()

    barrier = pltpu.get_barrier_semaphore()

    def greet(i, carry):
        chip = (z * 2 + lax.div(i, 8), lax.rem(i, 8) * 2)
        pl.semaphore_signal(barrier, inc=1, device_id=chip, device_id_type=MESH)
        return carry

    lax.fori_loop(0, n_blocks, greet, 0)
    beyond = (lax.rem(z + n_z - 1 + 2 * core, n_z) * 2 + xh, me_h - core + 1)
    pl.semaphore_signal(barrier, inc=1, device_id=beyond, device_id_type=MESH)

    def tell_other_core():
        pl.semaphore_signal(peer_sem, inc=1, device_id=(ctx, other), device_id_type=MESH)

    @pl.when(core == 0)
    def _():
        pl.semaphore_wait(barrier, 2 * n_blocks)
        tell_other_core()

    @pl.when(core == 1)
    def _():
        pl.semaphore_wait(peer_sem, 1)

    mine = xh == core

    def send(is_self, device, src, dst, send_sem, recv_sem):
        @pl.when(is_self)
        def _():
            pltpu.make_async_copy(src, dst, recv_sem).start()

        @pl.when(jnp.logical_not(is_self))
        def _():
            pltpu.make_async_remote_copy(
                src_ref=src, dst_ref=dst, send_sem=send_sem, recv_sem=recv_sem,
                device_id=device, device_id_type=MESH,
            ).start()

    key_rows = pl.ds(pl.multiple_of(WINDOW + me_h * BLOCK, BLOCK), BLOCK)

    def send_kv(i, carry):
        device, head = target(i)
        is_self = jnp.logical_and(mine, head == my_head)
        cols = pl.ds(pl.multiple_of(head * HEAD_WIDTH, HEAD_WIDTH), HEAD_WIDTH)
        send(is_self, device, k_ref.at[:, cols], kv.at[0, key_rows, :], s_k, r_kv.at[me_h])
        send(is_self, device, v_ref.at[:, cols], kv.at[1, key_rows, :], s_v, r_kv.at[me_h])
        return carry

    def send_qg(i, carry):
        device, head = target(i)
        is_self = jnp.logical_and(mine, head == my_head)
        cols = pl.ds(pl.multiple_of(head * 2 * HEAD_WIDTH, 2 * HEAD_WIDTH), 2 * HEAD_WIDTH)
        send(is_self, device, q_ref.at[:, cols], qg.at[me_h, 0], s_q, r_qg.at[me_h])
        send(is_self, device, g_ref.at[:, cols], qg.at[me_h, 1], s_g, r_qg.at[me_h])
        return carry

    lax.fori_loop(0, n_blocks, send_kv, 0)
    lax.fori_loop(0, n_blocks, send_qg, 0)

    dk[...] = jnp.zeros_like(dk)
    dv[...] = jnp.zeros_like(dv)

    @pl.when(core == 1)
    def _():
        pl.semaphore_wait(barrier, 2)
        tell_other_core()

    def take_kv(i, carry):
        h = source(i)
        rows = pl.ds(pl.multiple_of(WINDOW + h * BLOCK, BLOCK), BLOCK)
        bytes_of(kv.at[:, rows, :], r_kv.at[h]).wait()

        @pl.when(h >= half)
        def _():
            lead = pl.ds(pl.multiple_of((h - half) * BLOCK, BLOCK), BLOCK)
            pltpu.make_async_remote_copy(
                src_ref=kv.at[:, rows, :], dst_ref=kv.at[:, lead, :], send_sem=s_halo,
                recv_sem=r_halo, device_id=after, device_id_type=MESH,
            ).start()

        return carry

    lax.fori_loop(0, n_blocks, take_kv, 0)
    rows_mask.wait()
    bytes_of(kv.at[:, pl.ds(0, WINDOW), :], r_halo).wait()

    head_cols = pl.ds(pl.multiple_of(my_head * HEAD_WIDTH, HEAD_WIDTH), HEAD_WIDTH)
    pair_cols = pl.ds(pl.multiple_of(my_head * 2 * HEAD_WIDTH, 2 * HEAD_WIDTH), 2 * HEAD_WIDTH)

    def work(i, carry):
        h = source(i)
        bytes_of(qg.at[h], r_qg.at[h]).wait()
        bits = [
            (bits_ref[SPAN_BLOCKS - 1 - o, seg_lane + h] > 0) & (seg * n_blocks + h + o >= SPAN_BLOCKS - 1)
            for o in range(SPAN_BLOCKS)
        ]
        q2 = jnp.concatenate([qg[h, 0, :, :HEAD_WIDTH], qg[h, 0, :, HEAD_WIDTH:]], axis=0)
        g2 = jnp.concatenate([qg[h, 1, :, :HEAD_WIDTH], qg[h, 1, :, HEAD_WIDTH:]], axis=0)
        dq = block_grads(bits, h * BLOCK, q2, g2, kv, st, dp, pbs, dss, dk, dv)
        dqs[h] = jnp.concatenate([dq[:BLOCK], dq[BLOCK:]], axis=1).astype(BF16)
        is_self = jnp.logical_and(mine, h == me_h)
        send(is_self, (seg, h), dqs.at[h], dq_out.at[:, pair_cols], s_dq, r_dq)
        return carry

    lax.fori_loop(0, n_blocks, work, 0)

    halo_out[0] = (dk[pl.ds(0, WINDOW), :] * PRE_SCALE).astype(BF16)
    halo_out[1] = dv[pl.ds(0, WINDOW), :].astype(BF16)
    back = pltpu.make_async_remote_copy(
        src_ref=halo_out, dst_ref=halo_in, send_sem=s_back, recv_sem=r_back,
        device_id=before, device_id_type=MESH,
    )

    @pl.when(core == 0)
    def _():
        pl.semaphore_wait(peer_sem, 1)

    back.start()

    def send_dkv(h):
        is_self = jnp.logical_and(mine, h == me_h)
        send(is_self, (seg, h), dkvs.at[0, h], dk_out.at[:, head_cols], s_dk, r_dk)
        send(is_self, (seg, h), dkvs.at[1, h], dv_out.at[:, head_cols], s_dv, r_dv)

    def finish_low(h, carry):
        rows = pl.ds(pl.multiple_of(WINDOW + h * BLOCK, BLOCK), BLOCK)
        dkvs[0, h] = (dk[rows, :] * PRE_SCALE).astype(BF16)
        dkvs[1, h] = dv[rows, :].astype(BF16)
        send_dkv(h)
        return carry

    lax.fori_loop(0, half, finish_low, 0)
    back.wait_recv()

    def finish_high(h, carry):
        rows = pl.ds(pl.multiple_of(WINDOW + h * BLOCK, BLOCK), BLOCK)
        lead = pl.ds(pl.multiple_of((h - half) * BLOCK, BLOCK), BLOCK)
        dkvs[0, h] = (dk[rows, :] * PRE_SCALE + halo_in[0, lead, :].astype(F32)).astype(BF16)
        dkvs[1, h] = (dv[rows, :] + halo_in[1, lead, :].astype(F32)).astype(BF16)
        send_dkv(h)
        return carry

    lax.fori_loop(half, n_blocks, finish_high, 0)

    back.wait_send()
    bytes_of(kv.at[:, pl.ds(0, WINDOW), :], s_halo).wait()

    def sent(ref, width, sem):
        @pl.when(mine)
        def _():
            bytes_of(ref.at[:, pl.ds(0, (n_blocks - 1) * width)], sem).wait()

        @pl.when(jnp.logical_not(mine))
        def _():
            bytes_of(ref, sem).wait()

    for ref, width, sem in (
        (q_ref, 2 * HEAD_WIDTH, s_q),
        (g_ref, 2 * HEAD_WIDTH, s_g),
        (k_ref, HEAD_WIDTH, s_k),
        (v_ref, HEAD_WIDTH, s_v),
        (dq_out, 2 * HEAD_WIDTH, s_dq),
        (dk_out, HEAD_WIDTH, s_dk),
        (dv_out, HEAD_WIDTH, s_dv),
    ):
        sent(ref, width, sem)
    bytes_of(dq_out, r_dq).wait()
    bytes_of(dk_out, r_dk).wait()
    bytes_of(dv_out, r_dv).wait()


def put_out(a, b, c, a_out, b_out, c_out, a_sem, b_sem, c_sem):
    copies = [
        pltpu.make_async_copy(src, dst, sem)
        for src, dst, sem in ((a, a_out, a_sem), (b, b_out, b_sem), (c, c_out, c_sem))
    ]
    for copy in copies:
        copy.start()
    for copy in copies:
        copy.wait()


def solution(mesh):
    n_z = mesh.shape["ctx"] // 2
    n_blocks = mesh.shape["head"]

    def on_device(query, key, value, out_grad, block_mask):
        any_space = pl.BlockSpec(memory_space=pl.ANY)
        dma = pltpu.SemaphoreType.DMA
        keys = n_blocks * BLOCK + WINDOW
        cols = 2 * BLOCK

        def body(*refs):
            kernel(n_z, *refs)

        landed = pl.pallas_call(
            body,
            out_shape=(
                pltpu.VMEM(query.shape, BF16),
                pltpu.VMEM(key.shape, BF16),
                pltpu.VMEM(value.shape, BF16),
            ),
            in_specs=[any_space] * 5,
            out_specs=(pl.BlockSpec(memory_space=pltpu.VMEM),) * 3,
            scratch_shapes=[
                pltpu.VMEM((2, keys, HEAD_WIDTH), BF16),
                pltpu.VMEM((n_blocks, 2, BLOCK, 2 * HEAD_WIDTH), BF16),
                pltpu.VMEM((n_blocks, BLOCK, 2 * HEAD_WIDTH), BF16),
                pltpu.VMEM((2, n_blocks, BLOCK, HEAD_WIDTH), BF16),
                pltpu.VMEM((2, WINDOW, HEAD_WIDTH), BF16),
                pltpu.VMEM((2, WINDOW, HEAD_WIDTH), BF16),
                pltpu.VMEM((keys, HEAD_WIDTH), F32),
                pltpu.VMEM((keys, HEAD_WIDTH), F32),
                pltpu.VMEM((SPAN_BLOCKS, BLOCK, cols), F32),
                pltpu.VMEM((SPAN_BLOCKS, BLOCK, cols), F32),
                pltpu.VMEM((SPAN_BLOCKS * BLOCK, cols), BF16),
                pltpu.VMEM((SPAN_BLOCKS * BLOCK, cols), BF16),
                pltpu.SMEM((block_mask.shape[1], LANES), jnp.int32),
                dma, dma, dma, dma, dma((n_blocks,)), dma((n_blocks,)),
                dma, dma, dma, dma, dma, dma, dma, dma, dma, dma, dma,
                pltpu.SemaphoreType.REGULAR,
            ],
            compiler_params=pltpu.CompilerParams(collective_id=0, has_side_effects=True),
            name="window_attention_grads",
        )(query, key, value, out_grad, block_mask.T)
        return pl.pallas_call(
            put_out,
            out_shape=tuple(jax.ShapeDtypeStruct(a.shape, BF16) for a in (query, key, value)),
            in_specs=[any_space] * 3,
            out_specs=(any_space,) * 3,
            scratch_shapes=[dma, dma, dma],
            name="put_out",
            compiler_params=pltpu.CompilerParams(vmem_limit_bytes=2**20),
        )(*landed)

    tokens = P(("ctx", "head"), None)
    return jax.shard_map(
        on_device,
        mesh=mesh,
        in_specs=(tokens, tokens, tokens, tokens, P()),
        out_specs=(tokens, tokens, tokens),
        check_vma=False,
    )
```

```python
import math

import jax
import jax.numpy as jnp
from jax import lax
from jax.experimental import pallas as pl
from jax.experimental.pallas import tpu as pltpu
from jax.sharding import PartitionSpec as P

HEAD_WIDTH = 128
BLOCK = 128
LANES = 128
SPAN_BLOCKS = 9
CHUNK = 3
WINDOW = 1024
PRE_SCALE = 168.0 ** (-0.5)
EXP2_SCALE = PRE_SCALE / math.log(2.0)

F32 = jnp.float32
BF16 = jnp.bfloat16
MESH = pl.DeviceIdType.MESH

NT = (((1,), (1,)), ((), ()))
TN = (((0,), (0,)), ((), ()))
NN = (((1,), (0,)), ((), ()))


def dot(a, b, dims):
    return lax.dot_general(a, b, dims, preferred_element_type=F32)


def fold(x, op):
    return op(x.reshape(BLOCK // 8, 8, x.shape[1]), axis=0)


def bytes_of(ref, sem):
    return pltpu.make_async_copy(ref, ref, sem)


def block_grads(bits, first_row, q2, g2, kv, st, dp, pbs, dss, dk, dv):
    cols = q2.shape[0]
    u_index = lax.broadcasted_iota(jnp.int32, (BLOCK, cols), 0)
    t_index = lax.rem(lax.broadcasted_iota(jnp.int32, (BLOCK, cols), 1), BLOCK)
    causal = u_index <= t_index
    rows = CHUNK * BLOCK

    def span(c):
        return pl.ds(pl.multiple_of(first_row + c * rows, BLOCK), rows)

    m8 = jnp.full((8, cols), -jnp.inf, F32)
    for c in range(SPAN_BLOCKS // CHUNK):
        s = dot(kv[0, span(c), :], q2, NT)
        for i in range(CHUNK):
            o = c * CHUNK + i
            part = s[i * BLOCK : (i + 1) * BLOCK]
            if o == SPAN_BLOCKS - 1:
                part = jnp.where(causal, part, -jnp.inf)
            if o == 0:
                part = jnp.where(causal, -jnp.inf, part)
            st[o] = part
            m8 = jnp.maximum(m8, jnp.where(bits[o], fold(part, jnp.max), -jnp.inf))
    row_max = jnp.max(m8, axis=0, keepdims=True)

    l8 = jnp.zeros((8, cols), F32)
    d8 = jnp.zeros((8, cols), F32)
    for c in range(SPAN_BLOCKS // CHUNK):
        d = dot(kv[1, span(c), :], g2, NT)
        for i in range(CHUNK):
            o = c * CHUNK + i
            part = d[i * BLOCK : (i + 1) * BLOCK]
            shift = jnp.where(bits[o], row_max, jnp.inf)
            e = jnp.exp2((st[o] - shift) * EXP2_SCALE)
            st[o] = e
            dp[o] = part
            l8 += fold(e, jnp.sum)
            d8 += fold(e * part, jnp.sum)
    inverse = 1.0 / jnp.sum(l8, axis=0, keepdims=True)
    delta = jnp.sum(d8, axis=0, keepdims=True) * inverse

    dq = jnp.zeros((cols, HEAD_WIDTH), F32)
    for c in range(SPAN_BLOCKS // CHUNK):
        for i in range(CHUNK):
            o = c * CHUNK + i
            p = st[o] * inverse
            pbs[pl.ds(o * BLOCK, BLOCK), :] = p.astype(BF16)
            dss[pl.ds(o * BLOCK, BLOCK), :] = (p * (dp[o] - delta)).astype(BF16)
        pb = pbs[pl.ds(c * rows, rows), :]
        ds = dss[pl.ds(c * rows, rows), :]
        dv[span(c), :] += dot(pb, g2, NN)
        dk[span(c), :] += dot(ds, q2, NN)
        dq += dot(ds, kv[0, span(c), :], TN)
    return dq * PRE_SCALE


def kernel(
    n_z, q_ref, k_ref, v_ref, g_ref, mask_ref, dq_out, dk_out, dv_out,
    kv, qg, dqs, dkvs, halo_out, halo_in, dk, dv, st, dp, pbs, dss, bits_ref,
    s_q, s_g, s_k, s_v, r_qg, r_kv, s_halo, r_halo, s_back, r_back,
    s_dq, s_dk, s_dv, r_dq, r_dk, r_dv, m_sem, peer_sem,
):
    ctx = lax.axis_index("ctx")
    me_h = lax.axis_index("head")
    z, xh = lax.div(ctx, 2), lax.rem(ctx, 2)
    y, xl, core = lax.div(me_h, 4), lax.rem(lax.div(me_h, 2), 2), lax.rem(me_h, 2)
    x = xh * 2 + xl
    my_head = x * 4 + y
    seg = z * 2 + core
    n_blocks = qg.shape[0]
    half = n_blocks // 2
    other = me_h + 1 - 2 * core
    after = (lax.rem(z + core, n_z) * 2 + xh, other)
    before = (lax.rem(z + n_z - 1 + core, n_z) * 2 + xh, other)

    way = 1 - 2 * core

    def pair_step(pair):
        dx = lax.rem(pair, 2)
        return dx, lax.rem(lax.div(pair, 2) + 2 * dx, 4)

    def target(i):
        pair, second = lax.div(i, 2), lax.rem(i, 2)
        dx, dy = pair_step(pair)
        dx = dx + 2 * second
        tx, ty = lax.rem(x + 4 + way * dx, 4), lax.rem(y + 4 + way * dy, 4)
        return (z * 2 + lax.div(tx, 2), ty * 4 + lax.rem(tx, 2) * 2 + xh), tx * 4 + ty

    def source(i):
        pair, sc = lax.div(i, 2), lax.rem(i, 2)
        dx, dy = pair_step(pair)
        return lax.rem(y + 4 - (1 - 2 * sc) * dy, 4) * 4 + lax.rem(x + dx, 2) * 2 + sc

    lanes = bits_ref.shape[1]
    seg_lane = lax.rem(seg * n_blocks, lanes)
    lane_tile = pl.ds(pl.multiple_of(lax.div(seg * n_blocks, lanes) * lanes, lanes), lanes)
    rows_mask = pltpu.make_async_copy(mask_ref.at[:, lane_tile], bits_ref, m_sem)
    rows_mask.start()

    barrier = pltpu.get_barrier_semaphore()

    def greet(i, carry):
        chip = (z * 2 + lax.div(i, 8), lax.rem(i, 8) * 2)
        pl.semaphore_signal(barrier, inc=1, device_id=chip, device_id_type=MESH)
        return carry

    lax.fori_loop(0, n_blocks, greet, 0)
    beyond = (lax.rem(z + n_z - 1 + 2 * core, n_z) * 2 + xh, me_h - core + 1)
    pl.semaphore_signal(barrier, inc=1, device_id=beyond, device_id_type=MESH)

    def tell_other_core():
        pl.semaphore_signal(peer_sem, inc=1, device_id=(ctx, other), device_id_type=MESH)

    @pl.when(core == 0)
    def _():
        pl.semaphore_wait(barrier, 2 * n_blocks)
        tell_other_core()

    @pl.when(core == 1)
    def _():
        pl.semaphore_wait(peer_sem, 1)

    mine = xh == core

    def send(is_self, device, src, dst, send_sem, recv_sem):
        @pl.when(is_self)
        def _():
            pltpu.make_async_copy(src, dst, recv_sem).start()

        @pl.when(jnp.logical_not(is_self))
        def _():
            pltpu.make_async_remote_copy(
                src_ref=src, dst_ref=dst, send_sem=send_sem, recv_sem=recv_sem,
                device_id=device, device_id_type=MESH,
            ).start()

    key_rows = pl.ds(pl.multiple_of(WINDOW + me_h * BLOCK, BLOCK), BLOCK)

    def send_kv(i, carry):
        device, head = target(i)
        is_self = jnp.logical_and(mine, head == my_head)
        cols = pl.ds(pl.multiple_of(head * HEAD_WIDTH, HEAD_WIDTH), HEAD_WIDTH)
        send(is_self, device, k_ref.at[:, cols], kv.at[0, key_rows, :], s_k, r_kv.at[me_h])
        send(is_self, device, v_ref.at[:, cols], kv.at[1, key_rows, :], s_v, r_kv.at[me_h])
        return carry

    def send_qg(i, carry):
        device, head = target(i)
        is_self = jnp.logical_and(mine, head == my_head)
        cols = pl.ds(pl.multiple_of(head * 2 * HEAD_WIDTH, 2 * HEAD_WIDTH), 2 * HEAD_WIDTH)
        send(is_self, device, q_ref.at[:, cols], qg.at[me_h, 0], s_q, r_qg.at[me_h])
        send(is_self, device, g_ref.at[:, cols], qg.at[me_h, 1], s_g, r_qg.at[me_h])
        return carry

    lax.fori_loop(0, n_blocks, send_kv, 0)
    lax.fori_loop(0, n_blocks, send_qg, 0)

    dk[...] = jnp.zeros_like(dk)
    dv[...] = jnp.zeros_like(dv)

    @pl.when(core == 1)
    def _():
        pl.semaphore_wait(barrier, 2)
        tell_other_core()

    def take_kv(i, carry):
        h = source(i)
        rows = pl.ds(pl.multiple_of(WINDOW + h * BLOCK, BLOCK), BLOCK)
        bytes_of(kv.at[:, rows, :], r_kv.at[h]).wait()

        @pl.when(h >= half)
        def _():
            lead = pl.ds(pl.multiple_of((h - half) * BLOCK, BLOCK), BLOCK)
            pltpu.make_async_remote_copy(
                src_ref=kv.at[:, rows, :], dst_ref=kv.at[:, lead, :], send_sem=s_halo,
                recv_sem=r_halo, device_id=after, device_id_type=MESH,
            ).start()

        return carry

    lax.fori_loop(0, n_blocks, take_kv, 0)
    rows_mask.wait()
    bytes_of(kv.at[:, pl.ds(0, WINDOW), :], r_halo).wait()

    head_cols = pl.ds(pl.multiple_of(my_head * HEAD_WIDTH, HEAD_WIDTH), HEAD_WIDTH)
    pair_cols = pl.ds(pl.multiple_of(my_head * 2 * HEAD_WIDTH, 2 * HEAD_WIDTH), 2 * HEAD_WIDTH)

    back = pltpu.make_async_remote_copy(
        src_ref=halo_out, dst_ref=halo_in, send_sem=s_back, recv_sem=r_back,
        device_id=before, device_id_type=MESH,
    )

    def send_back():
        halo_out[0] = (dk[pl.ds(0, WINDOW), :] * PRE_SCALE).astype(BF16)
        halo_out[1] = dv[pl.ds(0, WINDOW), :].astype(BF16)

        @pl.when(core == 0)
        def _():
            pl.semaphore_wait(peer_sem, 1)

        back.start()

    last = n_blocks - 4

    def turn(i):
        m = lax.rem(i + 2 * lax.rem(lax.div(y + 1, 2), 2), 4)
        swapped = last + lax.div(m, 2) + lax.rem(m, 2) * (3 - 2 * lax.div(m, 2))
        return i + lax.div(i, last) * (swapped - i)

    def work(i, carry):
        pl.when(i == n_blocks - 2)(send_back)
        h = source(turn(i))
        bytes_of(qg.at[h], r_qg.at[h]).wait()
        bits = [
            (bits_ref[SPAN_BLOCKS - 1 - o, seg_lane + h] > 0) & (seg * n_blocks + h + o >= SPAN_BLOCKS - 1)
            for o in range(SPAN_BLOCKS)
        ]
        q2 = jnp.concatenate([qg[h, 0, :, :HEAD_WIDTH], qg[h, 0, :, HEAD_WIDTH:]], axis=0)
        g2 = jnp.concatenate([qg[h, 1, :, :HEAD_WIDTH], qg[h, 1, :, HEAD_WIDTH:]], axis=0)
        dq = block_grads(bits, h * BLOCK, q2, g2, kv, st, dp, pbs, dss, dk, dv)
        dqs[h] = jnp.concatenate([dq[:BLOCK], dq[BLOCK:]], axis=1).astype(BF16)
        is_self = jnp.logical_and(mine, h == me_h)
        send(is_self, (seg, h), dqs.at[h], dq_out.at[:, pair_cols], s_dq, r_dq)
        return carry

    lax.fori_loop(0, n_blocks, work, 0)

    def send_dkv(h):
        is_self = jnp.logical_and(mine, h == me_h)
        send(is_self, (seg, h), dkvs.at[0, h], dk_out.at[:, head_cols], s_dk, r_dk)
        send(is_self, (seg, h), dkvs.at[1, h], dv_out.at[:, head_cols], s_dv, r_dv)

    def finish_low(h, carry):
        rows = pl.ds(pl.multiple_of(WINDOW + h * BLOCK, BLOCK), BLOCK)
        dkvs[0, h] = (dk[rows, :] * PRE_SCALE).astype(BF16)
        dkvs[1, h] = dv[rows, :].astype(BF16)
        send_dkv(h)
        return carry

    lax.fori_loop(0, half, finish_low, 0)
    back.wait_recv()

    def finish_high(h, carry):
        rows = pl.ds(pl.multiple_of(WINDOW + h * BLOCK, BLOCK), BLOCK)
        lead = pl.ds(pl.multiple_of((h - half) * BLOCK, BLOCK), BLOCK)
        dkvs[0, h] = (dk[rows, :] * PRE_SCALE + halo_in[0, lead, :].astype(F32)).astype(BF16)
        dkvs[1, h] = (dv[rows, :] + halo_in[1, lead, :].astype(F32)).astype(BF16)
        send_dkv(h)
        return carry

    lax.fori_loop(half, n_blocks, finish_high, 0)

    back.wait_send()
    bytes_of(kv.at[:, pl.ds(0, WINDOW), :], s_halo).wait()

    def sent(ref, width, sem):
        @pl.when(mine)
        def _():
            bytes_of(ref.at[:, pl.ds(0, (n_blocks - 1) * width)], sem).wait()

        @pl.when(jnp.logical_not(mine))
        def _():
            bytes_of(ref, sem).wait()

    for ref, width, sem in (
        (q_ref, 2 * HEAD_WIDTH, s_q),
        (g_ref, 2 * HEAD_WIDTH, s_g),
        (k_ref, HEAD_WIDTH, s_k),
        (v_ref, HEAD_WIDTH, s_v),
        (dq_out, 2 * HEAD_WIDTH, s_dq),
        (dk_out, HEAD_WIDTH, s_dk),
        (dv_out, HEAD_WIDTH, s_dv),
    ):
        sent(ref, width, sem)
    bytes_of(dq_out, r_dq).wait()
    bytes_of(dk_out, r_dk).wait()
    bytes_of(dv_out, r_dv).wait()


def put_out(a, b, c, a_out, b_out, c_out, a_sem, b_sem, c_sem):
    copies = [
        pltpu.make_async_copy(src, dst, sem)
        for src, dst, sem in ((a, a_out, a_sem), (b, b_out, b_sem), (c, c_out, c_sem))
    ]
    for copy in copies:
        copy.start()
    for copy in copies:
        copy.wait()


def solution(mesh):
    n_z = mesh.shape["ctx"] // 2
    n_blocks = mesh.shape["head"]

    def on_device(query, key, value, out_grad, block_mask):
        any_space = pl.BlockSpec(memory_space=pl.ANY)
        dma = pltpu.SemaphoreType.DMA
        keys = n_blocks * BLOCK + WINDOW
        cols = 2 * BLOCK

        def body(*refs):
            kernel(n_z, *refs)

        landed = pl.pallas_call(
            body,
            out_shape=(
                pltpu.VMEM(query.shape, BF16),
                pltpu.VMEM(key.shape, BF16),
                pltpu.VMEM(value.shape, BF16),
            ),
            in_specs=[any_space] * 5,
            out_specs=(pl.BlockSpec(memory_space=pltpu.VMEM),) * 3,
            scratch_shapes=[
                pltpu.VMEM((2, keys, HEAD_WIDTH), BF16),
                pltpu.VMEM((n_blocks, 2, BLOCK, 2 * HEAD_WIDTH), BF16),
                pltpu.VMEM((n_blocks, BLOCK, 2 * HEAD_WIDTH), BF16),
                pltpu.VMEM((2, n_blocks, BLOCK, HEAD_WIDTH), BF16),
                pltpu.VMEM((2, WINDOW, HEAD_WIDTH), BF16),
                pltpu.VMEM((2, WINDOW, HEAD_WIDTH), BF16),
                pltpu.VMEM((keys, HEAD_WIDTH), F32),
                pltpu.VMEM((keys, HEAD_WIDTH), F32),
                pltpu.VMEM((SPAN_BLOCKS, BLOCK, cols), F32),
                pltpu.VMEM((SPAN_BLOCKS, BLOCK, cols), F32),
                pltpu.VMEM((SPAN_BLOCKS * BLOCK, cols), BF16),
                pltpu.VMEM((SPAN_BLOCKS * BLOCK, cols), BF16),
                pltpu.SMEM((block_mask.shape[1], LANES), jnp.int32),
                dma, dma, dma, dma, dma((n_blocks,)), dma((n_blocks,)),
                dma, dma, dma, dma, dma, dma, dma, dma, dma, dma, dma,
                pltpu.SemaphoreType.REGULAR,
            ],
            compiler_params=pltpu.CompilerParams(collective_id=0, has_side_effects=True),
            name="window_attention_grads",
        )(query, key, value, out_grad, block_mask.T)
        return pl.pallas_call(
            put_out,
            out_shape=tuple(jax.ShapeDtypeStruct(a.shape, BF16) for a in (query, key, value)),
            in_specs=[any_space] * 3,
            out_specs=(any_space,) * 3,
            scratch_shapes=[dma, dma, dma],
            name="put_out",
            compiler_params=pltpu.CompilerParams(vmem_limit_bytes=2**20),
        )(*landed)

    tokens = P(("ctx", "head"), None)
    return jax.shard_map(
        on_device,
        mesh=mesh,
        in_specs=(tokens, tokens, tokens, tokens, P()),
        out_specs=(tokens, tokens, tokens),
        check_vma=False,
    )
```

```python
import math

import jax
import jax.numpy as jnp
from jax import lax
from jax.experimental import pallas as pl
from jax.experimental.pallas import tpu as pltpu
from jax.sharding import PartitionSpec as P

HEAD_WIDTH = 128
BLOCK = 128
LANES = 128
SPAN_BLOCKS = 9
CHUNK = 3
WINDOW = 1024
PRE_SCALE = 168.0 ** (-0.5)
EXP2_SCALE = PRE_SCALE / math.log(2.0)

F32 = jnp.float32
BF16 = jnp.bfloat16
MESH = pl.DeviceIdType.MESH

NT = (((1,), (1,)), ((), ()))
TN = (((0,), (0,)), ((), ()))
NN = (((1,), (0,)), ((), ()))


def dot(a, b, dims):
    return lax.dot_general(a, b, dims, preferred_element_type=F32)


def fold(x, op):
    return op(x.reshape(BLOCK // 8, 8, x.shape[1]), axis=0)


def bytes_of(ref, sem):
    return pltpu.make_async_copy(ref, ref, sem)


def block_grads(bits, first_row, q2, g2, kv, st, dp, pbs, dss, dk, dv):
    cols = q2.shape[0]
    u_index = lax.broadcasted_iota(jnp.int32, (BLOCK, cols), 0)
    t_index = lax.rem(lax.broadcasted_iota(jnp.int32, (BLOCK, cols), 1), BLOCK)
    causal = u_index <= t_index
    rows = CHUNK * BLOCK

    def span(c):
        return pl.ds(pl.multiple_of(first_row + c * rows, BLOCK), rows)

    m8 = jnp.full((8, cols), -jnp.inf, F32)
    for c in range(SPAN_BLOCKS // CHUNK):
        s = dot(kv[0, span(c), :], q2, NT)
        for i in range(CHUNK):
            o = c * CHUNK + i
            part = s[i * BLOCK : (i + 1) * BLOCK]
            if o == SPAN_BLOCKS - 1:
                part = jnp.where(causal, part, -jnp.inf)
            if o == 0:
                part = jnp.where(causal, -jnp.inf, part)
            st[o] = part
            m8 = jnp.maximum(m8, jnp.where(bits[o], fold(part, jnp.max), -jnp.inf))
    row_max = jnp.max(m8, axis=0, keepdims=True)

    l8 = jnp.zeros((8, cols), F32)
    d8 = jnp.zeros((8, cols), F32)
    for c in range(SPAN_BLOCKS // CHUNK):
        d = dot(kv[1, span(c), :], g2, NT)
        for i in range(CHUNK):
            o = c * CHUNK + i
            part = d[i * BLOCK : (i + 1) * BLOCK]
            shift = jnp.where(bits[o], row_max, jnp.inf)
            e = jnp.exp2((st[o] - shift) * EXP2_SCALE)
            st[o] = e
            dp[o] = part
            l8 += fold(e, jnp.sum)
            d8 += fold(e * part, jnp.sum)
    inverse = 1.0 / jnp.sum(l8, axis=0, keepdims=True)
    delta = jnp.sum(d8, axis=0, keepdims=True) * inverse

    dq = jnp.zeros((cols, HEAD_WIDTH), F32)
    for c in range(SPAN_BLOCKS // CHUNK):
        for i in range(CHUNK):
            o = c * CHUNK + i
            p = st[o] * inverse
            pbs[pl.ds(o * BLOCK, BLOCK), :] = p.astype(BF16)
            dss[pl.ds(o * BLOCK, BLOCK), :] = (p * (dp[o] - delta)).astype(BF16)
        pb = pbs[pl.ds(c * rows, rows), :]
        ds = dss[pl.ds(c * rows, rows), :]
        dv[span(c), :] += dot(pb, g2, NN)
        dk[span(c), :] += dot(ds, q2, NN)
        dq += dot(ds, kv[0, span(c), :], TN)
    return dq * PRE_SCALE


def kernel(
    n_z, q_ref, k_ref, v_ref, g_ref, mask_ref, dq_out, dk_out, dv_out,
    kv, qg, dqs, dkvs, halo_out, halo_in, dk, dv, st, dp, pbs, dss, bits_ref,
    s_q, s_g, s_k, s_v, r_qg, r_kv, s_halo, r_halo, s_back, r_back,
    s_dq, s_dk, s_dv, r_dq, r_dk, r_dv, m_sem, peer_sem,
):
    ctx = lax.axis_index("ctx")
    me_h = lax.axis_index("head")
    z, xh = lax.div(ctx, 2), lax.rem(ctx, 2)
    y, xl, core = lax.div(me_h, 4), lax.rem(lax.div(me_h, 2), 2), lax.rem(me_h, 2)
    x = xh * 2 + xl
    my_head = x * 4 + y
    seg = z * 2 + core
    n_blocks = qg.shape[0]
    half = n_blocks // 2
    other = me_h + 1 - 2 * core
    after = (lax.rem(z + core, n_z) * 2 + xh, other)
    before = (lax.rem(z + n_z - 1 + core, n_z) * 2 + xh, other)

    way = 1 - 2 * core

    def pair_step(pair):
        dx = lax.rem(pair, 2)
        return dx, lax.rem(lax.div(pair, 2) + 2 * dx, 4)

    def target(i):
        pair, second = lax.div(i, 2), lax.rem(i, 2)
        dx, dy = pair_step(pair)
        dx = dx + 2 * second
        tx, ty = lax.rem(x + 4 + way * dx, 4), lax.rem(y + 4 + way * dy, 4)
        return (z * 2 + lax.div(tx, 2), ty * 4 + lax.rem(tx, 2) * 2 + xh), tx * 4 + ty

    def source(i):
        pair, sc = lax.div(i, 2), lax.rem(i, 2)
        dx, dy = pair_step(pair)
        return lax.rem(y + 4 - (1 - 2 * sc) * dy, 4) * 4 + lax.rem(x + dx, 2) * 2 + sc

    lanes = bits_ref.shape[1]
    seg_lane = lax.rem(seg * n_blocks, lanes)
    lane_tile = pl.ds(pl.multiple_of(lax.div(seg * n_blocks, lanes) * lanes, lanes), lanes)
    rows_mask = pltpu.make_async_copy(mask_ref.at[:, lane_tile], bits_ref, m_sem)
    rows_mask.start()

    barrier = pltpu.get_barrier_semaphore()

    def greet(i, carry):
        chip = (z * 2 + lax.div(i, 8), lax.rem(i, 8) * 2)
        pl.semaphore_signal(barrier, inc=1, device_id=chip, device_id_type=MESH)
        return carry

    lax.fori_loop(0, n_blocks, greet, 0)
    beyond = (lax.rem(z + n_z - 1 + 2 * core, n_z) * 2 + xh, me_h - core + 1)
    pl.semaphore_signal(barrier, inc=1, device_id=beyond, device_id_type=MESH)

    def tell_other_core():
        pl.semaphore_signal(peer_sem, inc=1, device_id=(ctx, other), device_id_type=MESH)

    @pl.when(core == 0)
    def _():
        pl.semaphore_wait(barrier, 2 * n_blocks)
        tell_other_core()

    @pl.when(core == 1)
    def _():
        pl.semaphore_wait(peer_sem, 1)

    mine = xh == core

    def send(is_self, device, src, dst, send_sem, recv_sem):
        @pl.when(is_self)
        def _():
            pltpu.make_async_copy(src, dst, recv_sem).start()

        @pl.when(jnp.logical_not(is_self))
        def _():
            pltpu.make_async_remote_copy(
                src_ref=src, dst_ref=dst, send_sem=send_sem, recv_sem=recv_sem,
                device_id=device, device_id_type=MESH,
            ).start()

    key_rows = pl.ds(pl.multiple_of(WINDOW + me_h * BLOCK, BLOCK), BLOCK)

    def send_kv(i, carry):
        device, head = target(i)
        is_self = jnp.logical_and(mine, head == my_head)
        cols = pl.ds(pl.multiple_of(head * HEAD_WIDTH, HEAD_WIDTH), HEAD_WIDTH)
        send(is_self, device, k_ref.at[:, cols], kv.at[0, key_rows, :], s_k, r_kv.at[me_h])
        send(is_self, device, v_ref.at[:, cols], kv.at[1, key_rows, :], s_v, r_kv.at[me_h])
        return carry

    def send_qg(i, carry):
        device, head = target(i)
        is_self = jnp.logical_and(mine, head == my_head)
        cols = pl.ds(pl.multiple_of(head * 2 * HEAD_WIDTH, 2 * HEAD_WIDTH), 2 * HEAD_WIDTH)
        send(is_self, device, q_ref.at[:, cols], qg.at[me_h, 0], s_q, r_qg.at[me_h])
        send(is_self, device, g_ref.at[:, cols], qg.at[me_h, 1], s_g, r_qg.at[me_h])
        return carry

    lax.fori_loop(0, n_blocks, send_kv, 0)
    lax.fori_loop(0, n_blocks, send_qg, 0)

    dk[...] = jnp.zeros_like(dk)
    dv[...] = jnp.zeros_like(dv)

    @pl.when(core == 1)
    def _():
        pl.semaphore_wait(barrier, 2)
        tell_other_core()

    def take_kv(i, carry):
        h = source(i)
        rows = pl.ds(pl.multiple_of(WINDOW + h * BLOCK, BLOCK), BLOCK)
        bytes_of(kv.at[:, rows, :], r_kv.at[h]).wait()

        @pl.when(h >= half)
        def _():
            lead = pl.ds(pl.multiple_of((h - half) * BLOCK, BLOCK), BLOCK)
            pltpu.make_async_remote_copy(
                src_ref=kv.at[:, rows, :], dst_ref=kv.at[:, lead, :], send_sem=s_halo,
                recv_sem=r_halo, device_id=after, device_id_type=MESH,
            ).start()

        return carry

    lax.fori_loop(0, n_blocks, take_kv, 0)
    rows_mask.wait()

    head_cols = pl.ds(pl.multiple_of(my_head * HEAD_WIDTH, HEAD_WIDTH), HEAD_WIDTH)
    pair_cols = pl.ds(pl.multiple_of(my_head * 2 * HEAD_WIDTH, 2 * HEAD_WIDTH), 2 * HEAD_WIDTH)

    back = pltpu.make_async_remote_copy(
        src_ref=halo_out, dst_ref=halo_in, send_sem=s_back, recv_sem=r_back,
        device_id=before, device_id_type=MESH,
    )

    def send_back():
        halo_out[0] = (dk[pl.ds(0, WINDOW), :] * PRE_SCALE).astype(BF16)
        halo_out[1] = dv[pl.ds(0, WINDOW), :].astype(BF16)

        @pl.when(core == 0)
        def _():
            pl.semaphore_wait(peer_sem, 1)

        back.start()

    last = n_blocks - 4

    def turn(i):
        first = lax.rem(i + 2 * (1 - lax.div(y, 2)), 4)
        early = lax.div(n_blocks + 3 - i, n_blocks)
        m = lax.rem(i + 2 * lax.rem(lax.div(y + 1, 2), 2), 4)
        swapped = last + lax.div(m, 2) + lax.rem(m, 2) * (3 - 2 * lax.div(m, 2))
        return i + lax.div(i, last) * (swapped - i) + early * (first - i)

    def work(i, carry):
        @pl.when(i == 2)
        def _():
            bytes_of(kv.at[:, pl.ds(0, WINDOW), :], r_halo).wait()

        pl.when(i == n_blocks - 2)(send_back)
        h = source(turn(i))
        bytes_of(qg.at[h], r_qg.at[h]).wait()
        bits = [
            (bits_ref[SPAN_BLOCKS - 1 - o, seg_lane + h] > 0) & (seg * n_blocks + h + o >= SPAN_BLOCKS - 1)
            for o in range(SPAN_BLOCKS)
        ]
        q2 = jnp.concatenate([qg[h, 0, :, :HEAD_WIDTH], qg[h, 0, :, HEAD_WIDTH:]], axis=0)
        g2 = jnp.concatenate([qg[h, 1, :, :HEAD_WIDTH], qg[h, 1, :, HEAD_WIDTH:]], axis=0)
        dq = block_grads(bits, h * BLOCK, q2, g2, kv, st, dp, pbs, dss, dk, dv)
        dqs[h] = jnp.concatenate([dq[:BLOCK], dq[BLOCK:]], axis=1).astype(BF16)
        is_self = jnp.logical_and(mine, h == me_h)
        send(is_self, (seg, h), dqs.at[h], dq_out.at[:, pair_cols], s_dq, r_dq)
        return carry

    lax.fori_loop(0, n_blocks, work, 0)

    def send_dkv(h):
        is_self = jnp.logical_and(mine, h == me_h)
        send(is_self, (seg, h), dkvs.at[0, h], dk_out.at[:, head_cols], s_dk, r_dk)
        send(is_self, (seg, h), dkvs.at[1, h], dv_out.at[:, head_cols], s_dv, r_dv)

    def finish_low(h, carry):
        rows = pl.ds(pl.multiple_of(WINDOW + h * BLOCK, BLOCK), BLOCK)
        dkvs[0, h] = (dk[rows, :] * PRE_SCALE).astype(BF16)
        dkvs[1, h] = dv[rows, :].astype(BF16)
        send_dkv(h)
        return carry

    lax.fori_loop(0, half, finish_low, 0)
    back.wait_recv()

    def finish_high(h, carry):
        rows = pl.ds(pl.multiple_of(WINDOW + h * BLOCK, BLOCK), BLOCK)
        lead = pl.ds(pl.multiple_of((h - half) * BLOCK, BLOCK), BLOCK)
        dkvs[0, h] = (dk[rows, :] * PRE_SCALE + halo_in[0, lead, :].astype(F32)).astype(BF16)
        dkvs[1, h] = (dv[rows, :] + halo_in[1, lead, :].astype(F32)).astype(BF16)
        send_dkv(h)
        return carry

    lax.fori_loop(half, n_blocks, finish_high, 0)

    back.wait_send()
    bytes_of(kv.at[:, pl.ds(0, WINDOW), :], s_halo).wait()

    def sent(ref, width, sem):
        @pl.when(mine)
        def _():
            bytes_of(ref.at[:, pl.ds(0, (n_blocks - 1) * width)], sem).wait()

        @pl.when(jnp.logical_not(mine))
        def _():
            bytes_of(ref, sem).wait()

    for ref, width, sem in (
        (q_ref, 2 * HEAD_WIDTH, s_q),
        (g_ref, 2 * HEAD_WIDTH, s_g),
        (k_ref, HEAD_WIDTH, s_k),
        (v_ref, HEAD_WIDTH, s_v),
        (dq_out, 2 * HEAD_WIDTH, s_dq),
        (dk_out, HEAD_WIDTH, s_dk),
        (dv_out, HEAD_WIDTH, s_dv),
    ):
        sent(ref, width, sem)
    bytes_of(dq_out, r_dq).wait()
    bytes_of(dk_out, r_dk).wait()
    bytes_of(dv_out, r_dv).wait()


def put_out(a, b, c, a_out, b_out, c_out, a_sem, b_sem, c_sem):
    copies = [
        pltpu.make_async_copy(src, dst, sem)
        for src, dst, sem in ((a, a_out, a_sem), (b, b_out, b_sem), (c, c_out, c_sem))
    ]
    for copy in copies:
        copy.start()
    for copy in copies:
        copy.wait()


def solution(mesh):
    n_z = mesh.shape["ctx"] // 2
    n_blocks = mesh.shape["head"]

    def on_device(query, key, value, out_grad, block_mask):
        any_space = pl.BlockSpec(memory_space=pl.ANY)
        dma = pltpu.SemaphoreType.DMA
        keys = n_blocks * BLOCK + WINDOW
        cols = 2 * BLOCK

        def body(*refs):
            kernel(n_z, *refs)

        landed = pl.pallas_call(
            body,
            out_shape=(
                pltpu.VMEM(query.shape, BF16),
                pltpu.VMEM(key.shape, BF16),
                pltpu.VMEM(value.shape, BF16),
            ),
            in_specs=[any_space] * 5,
            out_specs=(pl.BlockSpec(memory_space=pltpu.VMEM),) * 3,
            scratch_shapes=[
                pltpu.VMEM((2, keys, HEAD_WIDTH), BF16),
                pltpu.VMEM((n_blocks, 2, BLOCK, 2 * HEAD_WIDTH), BF16),
                pltpu.VMEM((n_blocks, BLOCK, 2 * HEAD_WIDTH), BF16),
                pltpu.VMEM((2, n_blocks, BLOCK, HEAD_WIDTH), BF16),
                pltpu.VMEM((2, WINDOW, HEAD_WIDTH), BF16),
                pltpu.VMEM((2, WINDOW, HEAD_WIDTH), BF16),
                pltpu.VMEM((keys, HEAD_WIDTH), F32),
                pltpu.VMEM((keys, HEAD_WIDTH), F32),
                pltpu.VMEM((SPAN_BLOCKS, BLOCK, cols), F32),
                pltpu.VMEM((SPAN_BLOCKS, BLOCK, cols), F32),
                pltpu.VMEM((SPAN_BLOCKS * BLOCK, cols), BF16),
                pltpu.VMEM((SPAN_BLOCKS * BLOCK, cols), BF16),
                pltpu.SMEM((block_mask.shape[1], LANES), jnp.int32),
                dma, dma, dma, dma, dma((n_blocks,)), dma((n_blocks,)),
                dma, dma, dma, dma, dma, dma, dma, dma, dma, dma, dma,
                pltpu.SemaphoreType.REGULAR,
            ],
            compiler_params=pltpu.CompilerParams(collective_id=0, has_side_effects=True),
            name="window_attention_grads",
        )(query, key, value, out_grad, block_mask.T)
        return pl.pallas_call(
            put_out,
            out_shape=tuple(jax.ShapeDtypeStruct(a.shape, BF16) for a in (query, key, value)),
            in_specs=[any_space] * 3,
            out_specs=(any_space,) * 3,
            scratch_shapes=[dma, dma, dma],
            name="put_out",
            compiler_params=pltpu.CompilerParams(vmem_limit_bytes=2**20),
        )(*landed)

    tokens = P(("ctx", "head"), None)
    return jax.shard_map(
        on_device,
        mesh=mesh,
        in_specs=(tokens, tokens, tokens, tokens, P()),
        out_specs=(tokens, tokens, tokens),
        check_vma=False,
    )
```
